256 devices in a mesh: rows: 64 (over x, z, core), rep: 4 (over y).
Axes of the slice: x: 4, y: 4, z: 8, core: 2. Of those that a mesh axis runs over, the one named last changes fastest.
Arguments:
- gallery: bfloat16 [65536, 1024], P('rows', 'rep'), may hold values from -6 to 6
- neighbours: int32 [65536, 10], P('rows'), may hold values from 0 to 65535, as said below
- queries: bfloat16 [128, 1024], P(None, 'rep'), may hold values from -6 to 6
- listed: int32 [128, 10], replicated, may hold values from 0 to 65535
Outputs:
- augmented: bfloat16 [65536, 1024], P('rows', 'rep')
- first_scores: float32 [128, 65536], P('rep', 'rows')
- final_scores: float32 [128, 65536], P('rep', 'rows')
The draws below stay inside these ranges and needn't reach their ends.
Inputs may be any that keep to these rules, and one draw needn't show every extreme that they name: `neighbours`: taking the rows in aligned blocks of 1024, the entries of one block name rows of another block at most 64 times and at most 32 distinct rows of it; in every draw one block is named exactly 64 times, at 32 distinct rows, by each other block.
All inputs are finite; a program needn't handle non-finite values.
Results may differ from the reference program's by a relative error of at most 0.017.
Values may be sent and summed in bfloat16 or wider, within the bound.
A program may use at most 64 MiB of HBM per device.

```python
import jax
import jax.numpy as jnp
from jax import lax

D = 1024
K = 10
KQ = 10
Q = 128
ROWS_DEV = 1024
CAP = 64
UCAP = 32
N = 65536


def draw_neighbours(key, part):
    blocks = N // ROWS_DEV
    keys = jax.random.split(key, 9)
    hottest = jax.random.randint(keys[0], (), 0, blocks)
    source = jnp.arange(blocks)[:, None]
    target = jnp.arange(blocks)[None, :]
    lowest = max(1, UCAP // 4)
    distinct = jax.random.randint(keys[1], (blocks, blocks), lowest, UCAP + 1)
    distinct = jnp.where(target == hottest, UCAP, distinct)
    spread = jax.random.randint(keys[2], (blocks, blocks), 0, CAP + 1)
    counts = distinct + spread * (CAP - distinct) // CAP
    counts = jnp.where(target == hottest, CAP, counts)
    counts = jnp.where(target == source, 0, counts)
    starting = jax.random.randint(keys[3], (blocks, blocks), 0, ROWS_DEV)
    primes = jnp.array([1299709, 15485863, 32452843], jnp.int32)
    chosen = jax.random.randint(keys[4], (blocks, blocks), 0, 3)
    stride = primes[chosen] % ROWS_DEV
    places = jnp.arange(CAP)[None, None, :]
    repeats = jax.random.randint(keys[5], (blocks, blocks, CAP), 0, UCAP) % distinct[..., None]
    which_row = jnp.where(places < distinct[..., None], places, repeats)
    offsets = (starting[..., None] + which_row * stride[..., None]) % ROWS_DEV
    remote_ids = target[..., None] * ROWS_DEV + offsets
    local_ids = source[..., None] * ROWS_DEV + jax.random.randint(keys[6], (blocks, blocks, CAP), 0, ROWS_DEV)
    grid = jnp.where(places < counts[..., None], remote_ids, local_ids).reshape(blocks, blocks * CAP)
    filler = source * ROWS_DEV + jax.random.randint(keys[7], (blocks, ROWS_DEV * K - blocks * CAP), 0, ROWS_DEV)
    entries = jnp.concatenate([grid, filler], axis=1)
    shuffled = jax.vmap(lambda row_key, row_ids: jax.random.permutation(row_key, row_ids))(jax.random.split(keys[8], blocks), entries)
    return shuffled.reshape(N, K).astype(jnp.int32)


def set_ends(result, rng, least, largest):
    shape = result.shape
    index_at = [jax.random.randint(jax.random.fold_in(rng, axis), (), 0, shape[axis]) for axis in range(len(shape))]
    result = result.at[tuple(index_at)].set(least)
    longest = shape.index(max(shape))
    index_at[longest] = (index_at[longest] + 1) % shape[longest]
    return result.at[tuple(index_at)].set(largest)


def level_of(key, shape, cuts, least, largest):
    loudness, own = 1.0, jax.random.fold_in(key, 6)
    for position, shards_of in cuts:
        draws = jnp.exp(jax.random.uniform(jax.random.fold_in(own, position), (shards_of,), jnp.float32, least / len(cuts), largest / len(cuts)))
        loudness = loudness * jnp.repeat(draws, shape[position] // shards_of).reshape([-1 if axis == position else 1 for axis in range(len(shape))])
    return loudness


def gaussian(stream_key, extent, scale, reach, cuts=(), kind=jnp.bfloat16):
    values = jax.random.normal(stream_key, extent, jnp.float32) * scale
    if len(cuts) > 0:
        values = level_of(stream_key, extent, cuts, -0.22, 0.18) * values
    return jnp.clip(values, min=-reach, max=reach).astype(kind)


def setup_inputs(seed: int = 0) -> dict:
    seeds = jax.random.split(jax.random.key(seed), 5)
    gallery = gaussian(seeds[0], (N, D), 1.0, 6.0, ((0, 64), (1, 4)))
    neighbours = draw_neighbours(jax.random.fold_in(seeds[4], 71), 0)
    queries = gaussian(seeds[2], (Q, D), 1.0, 6.0, ((1, 4),))
    listed = set_ends(jax.random.randint(seeds[3], (Q, KQ), 0, N), jax.random.fold_in(seeds[3], 1), 0, N - 1).astype(jnp.int32)
    return dict(gallery=gallery, neighbours=neighbours, queries=queries, listed=listed)


epsilon = 1e-06
logit_scale = 32.0

def reference(gallery, neighbours, queries, listed):
    link_count = neighbours.shape[1]
    row_total = gallery.shape[0]
    blocks = row_total // ROWS_DEV

    def augment_block(block_index):
        start = block_index * ROWS_DEV
        summed = lax.dynamic_slice_in_dim(gallery, start, ROWS_DEV, 0).astype(jnp.float32)
        links = lax.dynamic_slice_in_dim(neighbours, start, ROWS_DEV, 0)
        for column in range(link_count):
            weight = (2 * link_count - column) / (2 * link_count)
            summed = summed + weight * gallery[links[:, column]].astype(jnp.float32)
        rounded = summed.astype(jnp.bfloat16)
        widened = rounded.astype(jnp.float32)
        return (rounded, lax.optimization_barrier(jnp.sum(widened * widened, axis=1)))
    pieces, squares = lax.map(augment_block, jnp.arange(blocks, dtype=jnp.int32))
    augmented = pieces.reshape(row_total, -1)
    row_sq = squares.reshape(row_total)
    query_wide = queries.astype(jnp.float32)
    query_sq = lax.optimization_barrier(jnp.sum(query_wide * query_wide, axis=1))
    first_dot = jnp.dot(queries, augmented.T, preferred_element_type=jnp.float32)
    first_scores = logit_scale * first_dot * lax.rsqrt(query_sq + epsilon)[:, None] * lax.rsqrt(row_sq + epsilon)[None, :]
    listed_logit = jnp.take_along_axis(first_scores, listed, axis=1)
    weights = jnp.exp(listed_logit)
    unit_rows = augmented[listed].astype(jnp.float32) * lax.rsqrt(row_sq[listed] + epsilon)[..., None]
    numer = lax.optimization_barrier(jnp.sum(weights[..., None] * unit_rows, axis=1))
    denom = lax.optimization_barrier(jnp.sum(weights, axis=1))
    expanded = query_wide * lax.rsqrt(query_sq + epsilon)[:, None] + numer / denom[:, None]
    expanded_sq = lax.optimization_barrier(jnp.sum(expanded * expanded, axis=1))
    final_dot = jnp.dot(expanded.astype(jnp.bfloat16), augmented.T, preferred_element_type=jnp.float32)
    final_scores = logit_scale * final_dot * lax.rsqrt(expanded_sq + epsilon)[:, None] * lax.rsqrt(row_sq + epsilon)[None, :]
    return (augmented, first_scores, final_scores)
```

```python
import jax
import jax.numpy as jnp
from jax import lax
from jax.experimental import pallas as pl
from jax.experimental.pallas import tpu as pltpu
from jax.sharding import PartitionSpec as P

epsilon = 1e-06
logit_scale = 32.0
MESH = pl.DeviceIdType.MESH
f32, bf16, i32 = jnp.float32, jnp.bfloat16, jnp.int32

ROWS = 1024
COLS = 256
LINKS = 10
SLOTS = 32
XS, ZS, CS, YS = 4, 8, 2, 4
BLOCKS = XS * ZS * CS
QUERIES = 128
SHARE = QUERIES // YS
GROUP = 8
GROUPS = BLOCKS // GROUP


def split_offset(d):
    return d // (ZS * CS), (d // CS) % ZS, d % CS


def mirrored(d):
    dx, dz, dc = split_offset(d)
    return ((XS - dx) % XS) * (ZS * CS) + ((ZS - dz) % ZS) * CS + dc


def iota(shape, dim):
    return lax.broadcasted_iota(i32, shape, dim)


def dot(a, b, contract=((1,), (0,))):
    return lax.dot_general(a, b, (contract, ((), ())), preferred_element_type=f32)


def one_hot(mask):
    return jnp.where(mask, 1.0, 0.0).astype(bf16)


def wait_for(buffer, sem):
    pltpu.make_async_copy(buffer, buffer, sem).wait()


def kernel(
    gal_ref, nbt_ref, q_ref, lst_ref,
    aug_ref, first_ref, final_ref,
    nbb, cums, counts, req_out, req_in, cols, sel, picked, arrived, pick, acc, augt, rows_t, lsb,
    lsq_out, lsq_in, ft_out, ft_in, rsq_out, rsq_in,
    part, part_in, half, half_in, piece, whole, esq_out, esq_in, fp_out, fp_in, esq_col,
    send_req, recv_req, send_rep, recv_rep, send_y, recv_y, send_p, recv_p, send_e, recv_e,
):
    me = lax.axis_index("rows")
    my_y = lax.axis_index("rep")
    mx, mz, mc = me // (ZS * CS), (me // CS) % ZS, me % CS

    def peer(d):
        dx, dz, dc = split_offset(d)
        return ((mx + dx) % XS) * (ZS * CS) + ((mz + dz) % ZS) * CS + (mc + dc) % CS

    def send(src, dst, s_sem, r_sem, target):
        pltpu.make_async_remote_copy(
            src_ref=src, dst_ref=dst, send_sem=s_sem, recv_sem=r_sem,
            device_id=target, device_id_type=MESH,
        ).start()

    barrier = pltpu.get_barrier_semaphore()

    def greet(d, carry):
        pl.semaphore_signal(barrier, inc=1, device_id={"rows": peer(d)}, device_id_type=MESH)
        return carry

    lax.fori_loop(1, BLOCKS, greet, 0)
    for e in range(1, YS):
        pl.semaphore_signal(
            barrier, inc=1, device_id={"rep": (my_y + e) % YS}, device_id_type=MESH
        )

    wide = jnp.concatenate(
        [nbt_ref[...].astype(f32), jnp.zeros((128 - LINKS, ROWS), f32)], axis=0
    )
    for block in range(ROWS // 128):
        turned = jnp.transpose(wide[:, block * 128 : (block + 1) * 128]).astype(i32)
        for k in range(LINKS):
            nbb[k, block * 128 : (block + 1) * 128, :] = jnp.broadcast_to(
                turned[:, k : k + 1], (128, 128)
            )

    cums[...] = jnp.zeros_like(cums)

    def count_link(k, carry):
        row = nbt_ref[pl.ds(k, 1), :]
        total = jnp.zeros((256, 256), f32)
        for quarter in range(4):
            span = slice(quarter * 256, (quarter + 1) * 256)
            low = one_hot(iota((256, 256), 0) == (row[:, span] & 255))
            column = nbb[k, span, :] >> 8
            high = jnp.concatenate(
                [one_hot(iota((256, 128), 1) == column), one_hot(iota((256, 128), 1) + 128 == column)],
                axis=1,
            )
            total = total + dot(low, high)
        cums[...] += total
        return carry

    lax.fori_loop(0, LINKS, count_link, 0)

    def relative(high):
        block = high >> 2
        x, z, c = block >> 4, (block >> 1) & 7, block & 1
        return (((x - mx) & 3) << 4) | (((z - mz) & 7) << 1) | ((c - mc) & 1)

    high_row = iota((256, 256), 1)
    rel_row = relative(high_row)
    named = one_hot((cums[...] > 0.5) & (rel_row != 0))
    up_to = one_hot(iota((256, 256), 1) <= iota((256, 256), 0))
    earlier = one_hot(
        ((iota((256, 256), 0) >> 2) == (iota((256, 256), 1) >> 2))
        & (iota((256, 256), 0) < iota((256, 256), 1))
    )
    before = dot(jnp.ones((256, 256), bf16), named).astype(bf16)
    cums[...] = dot(up_to, named) + dot(before, earlier)
    for s in range(SLOTS):
        counts[pl.ds(s, 1), :] = jnp.sum(
            jnp.where(cums[...] <= float(s), 1.0, 0.0), axis=0, keepdims=True
        )
    count = jnp.concatenate([counts[...].astype(bf16)] * 4, axis=0)
    to_row = one_hot(iota((BLOCKS, 256), 0) == relative(iota((BLOCKS, 256), 1)))
    asked = dot(to_row, count, ((1,), (1,)))
    for d in range(BLOCKS):
        req_out[d] = asked[d : d + 1, :]

    pl.semaphore_wait(barrier, BLOCKS - 1 + YS - 1)

    def ask(d, carry):
        send(req_out.at[d], req_in.at[mirrored(d)], send_req, recv_req, {"rows": peer(d)})
        return carry

    lax.fori_loop(1, BLOCKS, ask, 0)

    quarter_of = (relative(iota((128, 256), 1)) & 3) == (iota((128, 256), 0) >> 5)
    four = jnp.where(quarter_of, count.astype(f32), 0.0).astype(bf16)
    chunks = BLOCKS * SLOTS // 128
    to_chunk = one_hot(iota((chunks, 256), 0) == (relative(iota((chunks, 256), 1)) >> 2))
    offset = dot(to_chunk, four, ((1,), (1,))).astype(i32)
    rel = iota((chunks, 128), 0) * 4 + (iota((chunks, 128), 1) >> 5)
    owner = (
        (((rel >> 4) + mx) & 3) * (ZS * CS) + ((((rel >> 1) & 7) + mz) & 7) * CS + ((rel + mc) & 1)
    )
    far_ids = jnp.where(offset < ROWS, owner * ROWS + offset, -1)
    near_ids = me * ROWS + iota((ROWS // 128, 128), 0) * 128 + iota((ROWS // 128, 128), 1)
    for c in range(ROWS // 128):
        cols[c] = jnp.broadcast_to(near_ids[c : c + 1, :], (8, 128))
    for c in range(chunks):
        cols[ROWS // 128 + c] = jnp.broadcast_to(far_ids[c : c + 1, :], (8, 128))
    arrived[0] = jnp.zeros((SLOTS, COLS), bf16)

    wait_for(req_in.at[pl.ds(1, BLOCKS - 1)], recv_req)
    wanted = jnp.concatenate(
        [req_in[d] if d else jnp.full((1, 128), float(ROWS), f32) for d in range(BLOCKS)]
        + [jnp.zeros((128 - BLOCKS, 128), f32)],
        axis=0,
    )
    wanted = jnp.transpose(wanted).astype(i32)
    for group in range(GROUPS):
        for j in range(GROUP):
            d = group * GROUP + j
            place = wanted[0:SLOTS, d : d + 1]
            pick[j * SLOTS : (j + 1) * SLOTS, :] = one_hot(iota((SLOTS, ROWS), 1) == place)
        taken = dot(pick[...], gal_ref[...]).astype(bf16)
        for j in range(GROUP):
            picked[group * GROUP + j] = taken[j * SLOTS : (j + 1) * SLOTS, :]
        for j in range(GROUP):
            d = group * GROUP + j
            if d:
                send(
                    picked.at[d], arrived.at[mirrored(d)], send_rep,
                    recv_rep.at[mirrored(d) // GROUP], {"rows": peer(d)},
                )

    def choose(block, carry):
        at = pl.multiple_of(block * 16, 16)
        ids = [nbb[k, pl.ds(at, 16), :] for k in range(LINKS)]
        for c in range(ROWS // 128 + chunks):
            column = cols[c]
            column = jnp.concatenate([column, column], axis=0)
            total = jnp.zeros((16, 128), f32)
            for k in range(LINKS):
                total = total + jnp.where(ids[k] == column, float(2 * LINKS - k), 0.0)
            sel[pl.ds(at, 16), c * 128 : (c + 1) * 128] = total.astype(bf16)
        return carry

    lax.fori_loop(0, ROWS // 16, choose, 0)
    acc[...] = float(2 * LINKS) * gal_ref[...].astype(f32)
    acc[...] += dot(sel[:, :ROWS], gal_ref[...])

    owned = lst_ref[...] >> 10
    inside = jnp.where(owned == me, lst_ref[...] & (ROWS - 1), -1)
    for k in range(LINKS):
        lsb[:, k * 128 : (k + 1) * 128] = one_hot(
            iota((ROWS, 128), 0) == inside[k : k + 1, :]
        )
    q_t = jnp.transpose(q_ref[...].astype(f32))
    query_sq = jnp.sum(q_t * q_t, axis=0, keepdims=True)

    for group in range(GROUPS):
        first_slot = 1 if group == 0 else group * GROUP
        last_slot = (group + 1) * GROUP
        wait_for(arrived.at[pl.ds(first_slot, last_slot - first_slot)], recv_rep.at[group])
        begin = ROWS + group * GROUP * SLOTS
        rows = arrived[group * GROUP : last_slot].reshape(GROUP * SLOTS, COLS)
        acc[...] += dot(sel[:, begin : begin + GROUP * SLOTS], rows)

    augmented = (acc[...] * (1.0 / (2 * LINKS))).astype(bf16)
    aug_ref[...] = augmented
    aug_t = jnp.transpose(augmented.astype(f32))
    augt[...] = aug_t.astype(bf16)

    def y_peer(e):
        return {"rep": (my_y + e) % YS}

    lsq_out[...] = jnp.zeros_like(lsq_out)
    for k in range(0, LINKS, 2):
        pair = dot(augt[...], lsb[:, k * 128 : (k + 2) * 128])
        rows_t[:, k * 128 : (k + 2) * 128] = pair
        for j in range(2):
            rows = pair[:, j * 128 : (j + 1) * 128]
            lsq_out[k + j : k + j + 1, :] = jnp.sum(rows * q_t, axis=0, keepdims=True)
            lsq_out[LINKS + k + j : LINKS + k + j + 1, :] = jnp.sum(
                rows * rows, axis=0, keepdims=True
            )
    lsq_out[2 * LINKS : 2 * LINKS + 1, :] = query_sq
    for e in (2, 1, 3):
        send(lsq_out, lsq_in.at[YS - e], send_y.at[0], recv_y.at[0], y_peer(e))

    row_sq = jnp.sum(aug_t * aug_t, axis=0, keepdims=True)
    rsq_out[...] = row_sq
    first = dot(q_ref[...], augt[...])
    for y in range(YS):
        ft_out[y] = first[y * SHARE : (y + 1) * SHARE, :].astype(bf16)
    for e in (2, 1, 3):
        send(rsq_out, rsq_in.at[YS - e], send_y.at[1], recv_y.at[1], y_peer(e))
        send(ft_out.at[(my_y + e) % YS], ft_in.at[YS - e], send_y.at[2], recv_y.at[2], y_peer(e))

    wait_for(lsq_in.at[pl.ds(1, YS - 1)], recv_y.at[0])
    sums = lsq_out[...] + lsq_in[1] + lsq_in[2] + lsq_in[3]
    q_scale = lax.rsqrt(sums[2 * LINKS : 2 * LINKS + 1, :] + epsilon)
    numer = jnp.zeros((COLS, QUERIES), f32)
    denom = jnp.zeros((1, QUERIES), f32)
    for k in range(LINKS):
        unit = lax.rsqrt(sums[LINKS + k : LINKS + k + 1, :] + epsilon)
        logit = logit_scale * sums[k : k + 1, :] * q_scale * unit
        weight = jnp.where(inside[k : k + 1, :] >= 0, jnp.exp(logit), 0.0)
        denom = denom + weight
        numer = numer + rows_t[:, k * 128 : (k + 1) * 128] * (weight * unit)

    def two_rows(total):
        high = total.astype(bf16).astype(f32)
        at = iota((16, QUERIES), 0)
        return jnp.where(at == 0, high, jnp.where(at == 1, total - high, 0.0)).astype(bf16)

    slice_rows = COLS // (XS * CS)
    tail = two_rows(denom)
    for i in range(XS * CS):
        part[i, 0:slice_rows] = numer[i * slice_rows : (i + 1) * slice_rows, :].astype(bf16)
        part[i, slice_rows:] = tail
    mine = mx * CS + mc

    def near(e):
        ex, ec = e // CS, e % CS
        return (mx + ex) % XS, (mc + ec) % CS, ((XS - ex) % XS) * CS + ec

    order = (4, 5, 2, 3, 6, 7, 1)
    for e in order:
        px, pc, back = near(e)
        send(
            part.at[px * CS + pc], part_in.at[back], send_p.at[0], recv_p.at[0],
            {"rows": px * (ZS * CS) + mz * CS + pc},
        )
    wait_for(part_in.at[pl.ds(1, XS * CS - 1)], recv_p.at[0])
    so_far = part[mine].astype(f32)
    for e in range(1, XS * CS):
        so_far = so_far + part_in[e].astype(f32)
    half[0:slice_rows] = so_far[0:slice_rows].astype(bf16)
    half[slice_rows:] = two_rows(so_far[slice_rows : slice_rows + 1] + so_far[slice_rows + 1 : slice_rows + 2])
    for e in (4, 3, 5, 2, 6, 1, 7):
        send(
            half, half_in.at[ZS - e], send_p.at[1], recv_p.at[1],
            {"rows": mx * (ZS * CS) + ((mz + e) % ZS) * CS + mc},
        )

    wait_for(rsq_in.at[pl.ds(1, YS - 1)], recv_y.at[1])
    wait_for(ft_in.at[pl.ds(1, YS - 1)], recv_y.at[2])
    row_scale = lax.rsqrt(rsq_out[...] + rsq_in[1] + rsq_in[2] + rsq_in[3] + epsilon)
    q_col = jnp.transpose(jnp.broadcast_to(q_scale * logit_scale, (QUERIES, QUERIES)))
    esq_col[...] = q_col
    mine_q = pl.ds(pl.multiple_of(my_y * SHARE, SHARE), SHARE)
    q_mine = esq_col[mine_q, 0:1]
    total = ft_out[my_y].astype(f32)
    for e in range(1, YS):
        total = total + ft_in[e].astype(f32)
    first_ref[...] = total * q_mine * row_scale

    wait_for(half_in.at[pl.ds(1, ZS - 1)], recv_p.at[1])
    so_far = half[...].astype(f32)
    for e in range(1, ZS):
        so_far = so_far + half_in[e].astype(f32)
    denom = so_far[slice_rows : slice_rows + 1] + so_far[slice_rows + 1 : slice_rows + 2]
    piece[...] = (so_far[0:slice_rows] / denom).astype(bf16)
    for e in order:
        px, pc, back = near(e)
        send(
            piece, whole.at[mine], send_p.at[2], recv_p.at[2],
            {"rows": px * (ZS * CS) + mz * CS + pc},
        )
    wait_for(whole.at[pl.ds(1, XS * CS - 1)], recv_p.at[2])
    whole[mine] = piece[...]

    expanded_t = q_t * q_scale + whole[...].reshape(COLS, QUERIES).astype(f32)
    esq_out[...] = jnp.sum(expanded_t * expanded_t, axis=0, keepdims=True)
    expanded = jnp.transpose(expanded_t).astype(bf16)
    final = dot(expanded, augt[...])
    for y in range(YS):
        fp_out[y] = final[y * SHARE : (y + 1) * SHARE, :].astype(bf16)
    for e in (2, 1, 3):
        send(esq_out, esq_in.at[YS - e], send_e.at[0], recv_e.at[0], y_peer(e))
        send(fp_out.at[(my_y + e) % YS], fp_in.at[YS - e], send_e.at[1], recv_e.at[1], y_peer(e))
    wait_for(esq_in.at[pl.ds(1, YS - 1)], recv_e.at[0])
    e_scale = lax.rsqrt(esq_out[...] + esq_in[1] + esq_in[2] + esq_in[3] + epsilon)
    esq_col[...] = jnp.transpose(jnp.broadcast_to(e_scale * logit_scale, (QUERIES, QUERIES)))
    e_mine = esq_col[mine_q, 0:1]
    wait_for(fp_in.at[pl.ds(1, YS - 1)], recv_e.at[1])
    total = fp_out[my_y].astype(f32)
    for e in range(1, YS):
        total = total + fp_in[e].astype(f32)
    final_ref[...] = total * e_mine * row_scale

    wait_for(req_out.at[pl.ds(1, BLOCKS - 1)], send_req)
    wait_for(picked.at[pl.ds(1, BLOCKS - 1)], send_rep)
    wait_for(lsq_in.at[pl.ds(1, YS - 1)], send_y.at[0])
    wait_for(rsq_in.at[pl.ds(1, YS - 1)], send_y.at[1])
    wait_for(ft_in.at[pl.ds(1, YS - 1)], send_y.at[2])
    wait_for(part_in.at[pl.ds(1, XS * CS - 1)], send_p.at[0])
    wait_for(half_in.at[pl.ds(1, ZS - 1)], send_p.at[1])
    wait_for(whole.at[pl.ds(1, XS * CS - 1)], send_p.at[2])
    wait_for(esq_in.at[pl.ds(1, YS - 1)], send_e.at[0])
    wait_for(fp_in.at[pl.ds(1, YS - 1)], send_e.at[1])


def local(gallery, neighbours, queries, listed):
    vmem = pl.BlockSpec(memory_space=pltpu.VMEM)
    slice_rows = COLS // (XS * CS)
    columns = ROWS + BLOCKS * SLOTS
    dma = pltpu.SemaphoreType.DMA
    return pl.pallas_call(
        kernel,
        out_shape=(
            jax.ShapeDtypeStruct((ROWS, COLS), bf16),
            jax.ShapeDtypeStruct((SHARE, ROWS), f32),
            jax.ShapeDtypeStruct((SHARE, ROWS), f32),
        ),
        in_specs=[vmem] * 4,
        out_specs=(vmem,) * 3,
        scratch_shapes=[
            pltpu.VMEM((LINKS, ROWS, 128), i32),
            pltpu.VMEM((256, 256), f32),
            pltpu.VMEM((SLOTS, 256), f32),
            pltpu.VMEM((BLOCKS, 1, 128), f32),
            pltpu.VMEM((BLOCKS, 1, 128), f32),
            pltpu.VMEM((columns // 128, 8, 128), i32),
            pltpu.VMEM((ROWS, columns), bf16),
            pltpu.VMEM((BLOCKS, SLOTS, COLS), bf16),
            pltpu.VMEM((BLOCKS, SLOTS, COLS), bf16),
            pltpu.VMEM((GROUP * SLOTS, ROWS), bf16),
            pltpu.VMEM((ROWS, COLS), f32),
            pltpu.VMEM((COLS, ROWS), bf16),
            pltpu.VMEM((COLS, LINKS * QUERIES), f32),
            pltpu.VMEM((ROWS, LINKS * QUERIES), bf16),
            pltpu.VMEM((24, QUERIES), f32),
            pltpu.VMEM((YS, 24, QUERIES), f32),
            pltpu.VMEM((YS, SHARE, ROWS), bf16),
            pltpu.VMEM((YS, SHARE, ROWS), bf16),
            pltpu.VMEM((1, ROWS), f32),
            pltpu.VMEM((YS, 1, ROWS), f32),
            pltpu.VMEM((XS * CS, slice_rows + 16, QUERIES), bf16),
            pltpu.VMEM((XS * CS, slice_rows + 16, QUERIES), bf16),
            pltpu.VMEM((slice_rows + 16, QUERIES), bf16),
            pltpu.VMEM((ZS, slice_rows + 16, QUERIES), bf16),
            pltpu.VMEM((slice_rows, QUERIES), bf16),
            pltpu.VMEM((XS * CS, slice_rows, QUERIES), bf16),
            pltpu.VMEM((1, QUERIES), f32),
            pltpu.VMEM((YS, 1, QUERIES), f32),
            pltpu.VMEM((YS, SHARE, ROWS), bf16),
            pltpu.VMEM((YS, SHARE, ROWS), bf16),
            pltpu.VMEM((QUERIES, QUERIES), f32),
            dma, dma, dma, dma((GROUPS,)), dma((3,)), dma((3,)), dma((3,)), dma((3,)), dma((2,)), dma((2,)),
        ],
        compiler_params=pltpu.CompilerParams(
            collective_id=0, has_side_effects=True, vmem_limit_bytes=60 * 1024 * 1024
        ),
        name="expand",
    )(gallery, neighbours.T, queries, listed.T)


def solution(mesh):
    return jax.shard_map(
        local,
        mesh=mesh,
        in_specs=(P("rows", "rep"), P("rows", None), P(None, "rep"), P()),
        out_specs=(P("rows", "rep"), P("rep", "rows"), P("rep", "rows")),
        check_vma=False,
    )
```

```python
import jax
import jax.numpy as jnp
from jax import lax
from jax.experimental import pallas as pl
from jax.experimental.pallas import tpu as pltpu
from jax.sharding import PartitionSpec as P

epsilon = 1e-06
logit_scale = 32.0
MESH = pl.DeviceIdType.MESH
f32, bf16, i32 = jnp.float32, jnp.bfloat16, jnp.int32

ROWS = 1024
COLS = 256
LINKS = 10
SLOTS = 32
XS, ZS, CS, YS = 4, 8, 2, 4
BLOCKS = XS * ZS * CS
QUERIES = 128
SHARE = QUERIES // YS
GROUP = 8
GROUPS = BLOCKS // GROUP
TAIL = 8


FAR_FIRST = (4, 3, 5, 2, 6, 1, 7, 0)
OWN = (ZS - 1) * XS * CS


def split_offset(slot):
    return (slot // CS) % XS, FAR_FIRST[slot // (XS * CS)], slot % CS


def mirrored(slot):
    dx, dz, dc = split_offset(slot)
    return FAR_FIRST.index((ZS - dz) % ZS) * (XS * CS) + ((XS - dx) % XS) * CS + dc


OTHERS = tuple(slot for slot in range(BLOCKS) if slot != OWN)


def iota(shape, dim):
    return lax.broadcasted_iota(i32, shape, dim)


def dot(a, b, contract=((1,), (0,))):
    return lax.dot_general(a, b, (contract, ((), ())), preferred_element_type=f32)


def one_hot(mask):
    return jnp.where(mask, 1.0, 0.0).astype(bf16)


def narrow_hot(mask):
    return jnp.where(mask, jnp.ones((), bf16), jnp.zeros((), bf16))


def wait_for(buffer, sem):
    pltpu.make_async_copy(buffer, buffer, sem).wait()


def kernel(
    gal_far, nbt_far, q_far, lst_far,
    aug_ref, first_ref, final_ref,
    gal_ref, nbt_ref, q_ref, lst_ref, nbb, cums, counts, req_out, req_in, cols, sel, picked, arrived, pick, acc, augt, rows_t, lsb,
    lsq_out, lsq_in, ft_out, ft_in, rsq_out, rsq_in,
    part, part_in, half, half_in, piece, whole, esq_out, esq_in, fp_out, fp_in, esq_col,
    sem_in, send_req, recv_req, send_rep, recv_rep, send_y, recv_y, send_p, recv_p, send_e, recv_e,
):
    me = lax.axis_index("rows")
    my_y = lax.axis_index("rep")
    mx, mz, mc = me // (ZS * CS), (me // CS) % ZS, me % CS

    at_x = [((mx + dx) % XS) * (ZS * CS) for dx in range(XS)]
    at_z = [((mz + dz) % ZS) * CS for dz in range(ZS)]
    at_c = [(mc + dc) % CS for dc in range(CS)]

    def peer(slot):
        dx, dz, dc = split_offset(slot)
        return {"rows": at_x[dx] + at_z[dz] + at_c[dc]}

    def send(src, dst, s_sem, r_sem, target):
        pltpu.make_async_remote_copy(
            src_ref=src, dst_ref=dst, send_sem=s_sem, recv_sem=r_sem,
            device_id=target, device_id_type=MESH,
        ).start()

    pairs = ((nbt_far, nbt_ref), (gal_far, gal_ref), (q_far, q_ref), (lst_far, lst_ref))
    bring = [pltpu.make_async_copy(a, b, sem_in.at[i]) for i, (a, b) in enumerate(pairs)]
    for copy in bring:
        copy.start()
    barrier = pltpu.get_barrier_semaphore()

    for slot in OTHERS:
        pl.semaphore_signal(barrier, inc=1, device_id=peer(slot), device_id_type=MESH)
    for e in range(1, YS):
        pl.semaphore_signal(
            barrier, inc=1, device_id={"rep": (my_y + e) % YS}, device_id_type=MESH
        )

    bring[0].wait()
    cums[...] = jnp.zeros_like(cums)

    places = iota((256, ROWS), 0).astype(f32).astype(bf16)

    def count_link(k, carry):
        row = nbt_ref[pl.ds(k, 1), :]
        low_row = (row & 255).astype(f32).astype(bf16)
        high_row = (row >> 8).astype(f32).astype(bf16)
        low = narrow_hot(places == low_row)
        high = narrow_hot(places == high_row)
        cums[...] += dot(low, high, ((1,), (1,)))
        return carry

    lax.fori_loop(0, LINKS, count_link, 0)

    def relative(high):
        block = high >> 2
        dx, dz, dc = ((block >> 4) - mx) & 3, ((block >> 1) - mz) & 7, (block - mc) & 1
        turn = jnp.where(dz > 4, 2 * (dz - 4), jnp.maximum(2 * (4 - dz) - 1, 0))
        return (turn << 3) | (dx << 1) | dc

    high_row = iota((256, 256), 1)
    rel_row = relative(high_row)
    named = one_hot((cums[...] > 0.5) & (rel_row != OWN))
    up_to = one_hot(iota((256, 256), 1) <= iota((256, 256), 0))
    earlier = one_hot(
        ((iota((256, 256), 0) >> 2) == (iota((256, 256), 1) >> 2))
        & (iota((256, 256), 0) < iota((256, 256), 1))
    )
    before = dot(jnp.ones((256, 256), bf16), named).astype(bf16)
    cums[...] = dot(up_to, named) + dot(before, earlier)
    narrow = jnp.minimum(cums[...], 255.0).astype(bf16)
    for s in range(SLOTS):
        under = narrow_hot(narrow <= float(s))
        while under.shape[0] > 16:
            under = under[: under.shape[0] // 2] + under[under.shape[0] // 2 :]
        counts[pl.ds(s, 1), :] = jnp.sum(under.astype(f32), axis=0, keepdims=True)
    count = jnp.concatenate([counts[...].astype(bf16)] * 4, axis=0)
    to_row = one_hot(iota((BLOCKS, 256), 0) == relative(iota((BLOCKS, 256), 1)))
    asked = dot(to_row, count, ((1,), (1,)))
    for slot in OTHERS:
        req_out[slot] = asked[slot : slot + 1, :]

    pl.semaphore_wait(barrier, BLOCKS - 1 + YS - 1)

    for slot in OTHERS:
        send(req_out.at[slot], req_in.at[mirrored(slot)], send_req, recv_req, peer(slot))

    wide = jnp.concatenate(
        [nbt_ref[...].astype(f32), jnp.zeros((128 - LINKS, ROWS), f32)], axis=0
    )
    for block in range(ROWS // 128):
        turned = jnp.transpose(wide[:, block * 128 : (block + 1) * 128]).astype(i32)
        for k in range(LINKS):
            nbb[k, block * 128 : (block + 1) * 128, :] = jnp.broadcast_to(
                turned[:, k : k + 1], (128, 128)
            )


    quarter_of = (relative(iota((128, 256), 1)) & 3) == (iota((128, 256), 0) >> 5)
    four = jnp.where(quarter_of, count.astype(f32), 0.0).astype(bf16)
    chunks = BLOCKS * SLOTS // 128
    to_chunk = one_hot(iota((chunks, 256), 0) == (relative(iota((chunks, 256), 1)) >> 2))
    offset = dot(to_chunk, four, ((1,), (1,))).astype(i32)
    slots = iota((chunks, 128), 0) * 4 + (iota((chunks, 128), 1) >> 5)
    turn = slots >> 3
    dz = jnp.where(turn == 7, 0, jnp.where((turn & 1) == 0, 4 + (turn >> 1), 4 - ((turn + 1) >> 1)))
    owner = (
        ((((slots >> 1) & 3) + mx) & 3) * (ZS * CS) + ((dz + mz) & 7) * CS + ((slots + mc) & 1)
    )
    far_ids = jnp.where(offset < ROWS, owner * ROWS + offset, -1)
    near_ids = me * ROWS + iota((ROWS // 128, 128), 0) * 128 + iota((ROWS // 128, 128), 1)
    for c in range(ROWS // 128):
        cols[c] = jnp.broadcast_to(near_ids[c : c + 1, :], (8, 128))
    for c in range(chunks):
        cols[ROWS // 128 + c] = jnp.broadcast_to(far_ids[c : c + 1, :], (8, 128))
    arrived[OWN] = jnp.zeros((SLOTS, COLS), bf16)
    for copy in bring[1:]:
        copy.wait()

    wait_for(req_in.at[pl.ds(0, BLOCKS - 1)], recv_req)
    wanted = jnp.concatenate(
        [req_in[d] if d != OWN else jnp.full((1, 128), float(ROWS), f32) for d in range(BLOCKS)]
        + [jnp.zeros((128 - BLOCKS, 128), f32)],
        axis=0,
    )
    wanted = jnp.transpose(wanted).astype(i32)
    for group in range(GROUPS):
        for j in range(GROUP):
            d = group * GROUP + j
            place = wanted[0:SLOTS, d : d + 1]
            pick[j * SLOTS : (j + 1) * SLOTS, :] = one_hot(iota((SLOTS, ROWS), 1) == place)
        taken = dot(pick[...], gal_ref[...]).astype(bf16)
        for j in range(GROUP):
            picked[group * GROUP + j] = taken[j * SLOTS : (j + 1) * SLOTS, :]
        for slot in range(group * GROUP, (group + 1) * GROUP):
            if slot != OWN:
                send(
                    picked.at[slot], arrived.at[mirrored(slot)], send_rep,
                    recv_rep.at[mirrored(slot) // GROUP], peer(slot),
                )

    def choose(block, carry):
        at = pl.multiple_of(block * 16, 16)
        ids = [nbb[k, pl.ds(at, 16), :] for k in range(LINKS)]
        for c in range(ROWS // 128 + chunks):
            column = cols[c]
            column = jnp.concatenate([column, column], axis=0)
            total = jnp.zeros((16, 128), f32)
            for k in range(LINKS):
                total = total + jnp.where(ids[k] == column, float(2 * LINKS - k), 0.0)
            sel[pl.ds(at, 16), c * 128 : (c + 1) * 128] = total.astype(bf16)
        return carry

    lax.fori_loop(0, ROWS // 16, choose, 0)
    acc[...] = float(2 * LINKS) * gal_ref[...].astype(f32)
    acc[...] += dot(sel[:, :ROWS], gal_ref[...])

    owned = lst_ref[...] >> 10
    inside = jnp.where(owned == me, lst_ref[...] & (ROWS - 1), -1)
    for k in range(LINKS):
        lsb[:, k * 128 : (k + 1) * 128] = one_hot(
            iota((ROWS, 128), 0) == inside[k : k + 1, :]
        )
    q_t = jnp.transpose(q_ref[...].astype(f32))
    query_sq = jnp.sum(q_t * q_t, axis=0, keepdims=True)

    for group in range(GROUPS):
        coming = GROUP - (OWN // GROUP == group)
        wait_for(arrived.at[pl.ds(group * GROUP, coming)], recv_rep.at[group])
        begin = ROWS + group * GROUP * SLOTS
        rows = arrived[group * GROUP : (group + 1) * GROUP].reshape(GROUP * SLOTS, COLS)
        acc[...] += dot(sel[:, begin : begin + GROUP * SLOTS], rows)

    augmented = (acc[...] * (1.0 / (2 * LINKS))).astype(bf16)
    aug_ref[...] = augmented
    aug_t = jnp.transpose(augmented.astype(f32))
    augt[...] = aug_t.astype(bf16)

    def y_peer(e):
        return {"rep": (my_y + e) % YS}

    lsq_out[...] = jnp.zeros_like(lsq_out)
    for k in range(0, LINKS, 2):
        pair = dot(augt[...], lsb[:, k * 128 : (k + 2) * 128])
        rows_t[:, k * 128 : (k + 2) * 128] = pair
        for j in range(2):
            rows = pair[:, j * 128 : (j + 1) * 128]
            lsq_out[k + j : k + j + 1, :] = jnp.sum(rows * q_t, axis=0, keepdims=True)
            lsq_out[LINKS + k + j : LINKS + k + j + 1, :] = jnp.sum(
                rows * rows, axis=0, keepdims=True
            )
    lsq_out[2 * LINKS : 2 * LINKS + 1, :] = query_sq
    for e in (2, 1, 3):
        send(lsq_out, lsq_in.at[YS - e], send_y.at[0], recv_y.at[0], y_peer(e))

    row_sq = jnp.sum(aug_t * aug_t, axis=0, keepdims=True)
    rsq_out[...] = row_sq
    first = dot(q_ref[...], augt[...])
    for y in range(YS):
        ft_out[y] = first[y * SHARE : (y + 1) * SHARE, :].astype(bf16)
    for e in (2, 1, 3):
        send(rsq_out, rsq_in.at[YS - e], send_y.at[1], recv_y.at[1], y_peer(e))
        send(ft_out.at[(my_y + e) % YS], ft_in.at[YS - e], send_y.at[2], recv_y.at[2], y_peer(e))

    wait_for(lsq_in.at[pl.ds(1, YS - 1)], recv_y.at[0])
    sums = lsq_out[...] + lsq_in[1] + lsq_in[2] + lsq_in[3]
    q_scale = lax.rsqrt(sums[2 * LINKS : 2 * LINKS + 1, :] + epsilon)
    numer = jnp.zeros((COLS, QUERIES), f32)
    denom = jnp.zeros((1, QUERIES), f32)
    for k in range(LINKS):
        unit = lax.rsqrt(sums[LINKS + k : LINKS + k + 1, :] + epsilon)
        logit = logit_scale * sums[k : k + 1, :] * q_scale * unit
        weight = jnp.where(inside[k : k + 1, :] >= 0, jnp.exp(logit), 0.0)
        denom = denom + weight
        numer = numer + rows_t[:, k * 128 : (k + 1) * 128] * (weight * unit)

    def two_rows(total):
        high = total.astype(bf16).astype(f32)
        at = iota((TAIL, QUERIES), 0)
        return jnp.where(at == 0, high, jnp.where(at == 1, total - high, 0.0)).astype(bf16)

    slice_rows = COLS // (XS * CS)
    tail = two_rows(denom)
    for i in range(XS * CS):
        part[i, 0:slice_rows] = numer[i * slice_rows : (i + 1) * slice_rows, :].astype(bf16)
        part[i, slice_rows:] = tail
    mine = mx * CS + mc

    def near(e):
        ex, ec = e // CS, e % CS
        return (mx + ex) % XS, (mc + ec) % CS, ((XS - ex) % XS) * CS + ec

    order = (4, 5, 2, 3, 6, 7, 1)
    for e in order:
        px, pc, back = near(e)
        send(
            part.at[px * CS + pc], part_in.at[back], send_p.at[0], recv_p.at[0],
            {"rows": px * (ZS * CS) + mz * CS + pc},
        )
    wait_for(part_in.at[pl.ds(1, XS * CS - 1)], recv_p.at[0])
    so_far = part[mine].astype(f32)
    for e in range(1, XS * CS):
        so_far = so_far + part_in[e].astype(f32)
    half[0:slice_rows] = so_far[0:slice_rows].astype(bf16)
    half[slice_rows:] = two_rows(so_far[slice_rows : slice_rows + 1] + so_far[slice_rows + 1 : slice_rows + 2])
    for e in (4, 3, 5, 2, 6, 1, 7):
        send(
            half, half_in.at[ZS - e], send_p.at[1], recv_p.at[1],
            {"rows": mx * (ZS * CS) + ((mz + e) % ZS) * CS + mc},
        )

    wait_for(rsq_in.at[pl.ds(1, YS - 1)], recv_y.at[1])
    wait_for(ft_in.at[pl.ds(1, YS - 1)], recv_y.at[2])
    row_scale = lax.rsqrt(rsq_out[...] + rsq_in[1] + rsq_in[2] + rsq_in[3] + epsilon)
    q_col = jnp.transpose(jnp.broadcast_to(q_scale * logit_scale, (QUERIES, QUERIES)))
    esq_col[...] = q_col
    mine_q = pl.ds(pl.multiple_of(my_y * SHARE, SHARE), SHARE)
    q_mine = esq_col[mine_q, 0:1]
    total = ft_out[my_y].astype(f32)
    for e in range(1, YS):
        total = total + ft_in[e].astype(f32)
    first_ref[...] = total * q_mine * row_scale

    wait_for(half_in.at[pl.ds(1, ZS - 1)], recv_p.at[1])
    so_far = half[...].astype(f32)
    for e in range(1, ZS):
        so_far = so_far + half_in[e].astype(f32)
    denom = so_far[slice_rows : slice_rows + 1] + so_far[slice_rows + 1 : slice_rows + 2]
    piece[...] = (so_far[0:slice_rows] / denom).astype(bf16)
    for e in order:
        px, pc, back = near(e)
        send(
            piece, whole.at[mine], send_p.at[2], recv_p.at[2],
            {"rows": px * (ZS * CS) + mz * CS + pc},
        )
    wait_for(whole.at[pl.ds(1, XS * CS - 1)], recv_p.at[2])
    whole[mine] = piece[...]

    expanded_t = q_t * q_scale + whole[...].reshape(COLS, QUERIES).astype(f32)
    esq_out[...] = jnp.sum(expanded_t * expanded_t, axis=0, keepdims=True)
    expanded = jnp.transpose(expanded_t).astype(bf16)
    final = dot(expanded, augt[...])
    for y in range(YS):
        fp_out[y] = final[y * SHARE : (y + 1) * SHARE, :].astype(bf16)
    for e in (2, 1, 3):
        send(esq_out, esq_in.at[YS - e], send_e.at[0], recv_e.at[0], y_peer(e))
        send(fp_out.at[(my_y + e) % YS], fp_in.at[YS - e], send_e.at[1], recv_e.at[1], y_peer(e))
    wait_for(esq_in.at[pl.ds(1, YS - 1)], recv_e.at[0])
    e_scale = lax.rsqrt(esq_out[...] + esq_in[1] + esq_in[2] + esq_in[3] + epsilon)
    esq_col[...] = jnp.transpose(jnp.broadcast_to(e_scale * logit_scale, (QUERIES, QUERIES)))
    e_mine = esq_col[mine_q, 0:1]
    wait_for(fp_in.at[pl.ds(1, YS - 1)], recv_e.at[1])
    total = fp_out[my_y].astype(f32)
    for e in range(1, YS):
        total = total + fp_in[e].astype(f32)
    final_ref[...] = total * e_mine * row_scale

    wait_for(req_out.at[pl.ds(0, BLOCKS - 1)], send_req)
    wait_for(picked.at[pl.ds(0, BLOCKS - 1)], send_rep)
    wait_for(lsq_in.at[pl.ds(1, YS - 1)], send_y.at[0])
    wait_for(rsq_in.at[pl.ds(1, YS - 1)], send_y.at[1])
    wait_for(ft_in.at[pl.ds(1, YS - 1)], send_y.at[2])
    wait_for(part_in.at[pl.ds(1, XS * CS - 1)], send_p.at[0])
    wait_for(half_in.at[pl.ds(1, ZS - 1)], send_p.at[1])
    wait_for(whole.at[pl.ds(1, XS * CS - 1)], send_p.at[2])
    wait_for(esq_in.at[pl.ds(1, YS - 1)], send_e.at[0])
    wait_for(fp_in.at[pl.ds(1, YS - 1)], send_e.at[1])


def hand_over(aug_in, first_in, final_in, aug_out, first_out, final_out, sems):
    pairs = ((aug_in, aug_out), (first_in, first_out), (final_in, final_out))
    copies = [pltpu.make_async_copy(a, b, sems.at[i]) for i, (a, b) in enumerate(pairs)]
    for copy in copies:
        copy.start()
    for copy in copies:
        copy.wait()


def local(gallery, neighbours, queries, listed):
    vmem = pl.BlockSpec(memory_space=pltpu.VMEM)
    slice_rows = COLS // (XS * CS)
    columns = ROWS + BLOCKS * SLOTS
    dma = pltpu.SemaphoreType.DMA
    results = (
        jax.ShapeDtypeStruct((ROWS, COLS), bf16),
        jax.ShapeDtypeStruct((SHARE, ROWS), f32),
        jax.ShapeDtypeStruct((SHARE, ROWS), f32),
    )
    made = pl.pallas_call(
        kernel,
        out_shape=tuple(pltpu.VMEM(r.shape, r.dtype) for r in results),
        in_specs=[pl.BlockSpec(memory_space=pltpu.HBM)] * 4,
        out_specs=(vmem,) * 3,
        scratch_shapes=[
            pltpu.VMEM((ROWS, COLS), bf16),
            pltpu.VMEM((LINKS, ROWS), i32),
            pltpu.VMEM((QUERIES, COLS), bf16),
            pltpu.VMEM((LINKS, QUERIES), i32),
            pltpu.VMEM((LINKS, ROWS, 128), i32),
            pltpu.VMEM((256, 256), f32),
            pltpu.VMEM((SLOTS, 256), f32),
            pltpu.VMEM((BLOCKS, 1, 128), f32),
            pltpu.VMEM((BLOCKS, 1, 128), f32),
            pltpu.VMEM((columns // 128, 8, 128), i32),
            pltpu.VMEM((ROWS, columns), bf16),
            pltpu.VMEM((BLOCKS, SLOTS, COLS), bf16),
            pltpu.VMEM((BLOCKS, SLOTS, COLS), bf16),
            pltpu.VMEM((GROUP * SLOTS, ROWS), bf16),
            pltpu.VMEM((ROWS, COLS), f32),
            pltpu.VMEM((COLS, ROWS), bf16),
            pltpu.VMEM((COLS, LINKS * QUERIES), f32),
            pltpu.VMEM((ROWS, LINKS * QUERIES), bf16),
            pltpu.VMEM((24, QUERIES), f32),
            pltpu.VMEM((YS, 24, QUERIES), f32),
            pltpu.VMEM((YS, SHARE, ROWS), bf16),
            pltpu.VMEM((YS, SHARE, ROWS), bf16),
            pltpu.VMEM((1, ROWS), f32),
            pltpu.VMEM((YS, 1, ROWS), f32),
            pltpu.VMEM((XS * CS, slice_rows + TAIL, QUERIES), bf16),
            pltpu.VMEM((XS * CS, slice_rows + TAIL, QUERIES), bf16),
            pltpu.VMEM((slice_rows + TAIL, QUERIES), bf16),
            pltpu.VMEM((ZS, slice_rows + TAIL, QUERIES), bf16),
            pltpu.VMEM((slice_rows, QUERIES), bf16),
            pltpu.VMEM((XS * CS, slice_rows, QUERIES), bf16),
            pltpu.VMEM((1, QUERIES), f32),
            pltpu.VMEM((YS, 1, QUERIES), f32),
            pltpu.VMEM((YS, SHARE, ROWS), bf16),
            pltpu.VMEM((YS, SHARE, ROWS), bf16),
            pltpu.VMEM((QUERIES, QUERIES), f32),
            dma((4,)), dma, dma, dma, dma((GROUPS,)), dma((3,)), dma((3,)), dma((3,)), dma((3,)), dma((2,)), dma((2,)),
        ],
        compiler_params=pltpu.CompilerParams(
            collective_id=0, has_side_effects=True, vmem_limit_bytes=66100000
        ),
        name="expand",
    )(gallery, neighbours.T, queries, listed.T)
    return pl.pallas_call(
        hand_over,
        out_shape=results,
        in_specs=[vmem] * 3,
        out_specs=(pl.BlockSpec(memory_space=pl.ANY),) * 3,
        scratch_shapes=[dma((3,))],
        compiler_params=pltpu.CompilerParams(vmem_limit_bytes=4 * 1024 * 1024),
        name="hand_over",
    )(*made)


def solution(mesh):
    return jax.shard_map(
        local,
        mesh=mesh,
        in_specs=(P("rows", "rep"), P("rows", None), P(None, "rep"), P()),
        out_specs=(P("rows", "rep"), P("rep", "rows"), P("rep", "rows")),
        check_vma=False,
    )
```

```python
import jax
import jax.numpy as jnp
from jax import lax
from jax.experimental import pallas as pl
from jax.experimental.pallas import tpu as pltpu
from jax.sharding import PartitionSpec as P

epsilon = 1e-06
logit_scale = 32.0
MESH = pl.DeviceIdType.MESH
f32, bf16, i32 = jnp.float32, jnp.bfloat16, jnp.int32

ROWS = 1024
COLS = 256
LINKS = 10
SLOTS = 32
XS, ZS, CS, YS = 4, 8, 2, 4
BLOCKS = XS * ZS * CS
QUERIES = 128
SHARE = QUERIES // YS
GROUP = 8
GROUPS = BLOCKS // GROUP
TAIL = 8


STEPS = (1, 7, 4, 3, 5, 2, 6, 0)
OWN = (ZS - 1) * XS * CS


def split_offset(slot):
    return (slot // CS) % XS, STEPS[slot // (XS * CS)], slot % CS


def mirrored(slot):
    dx, dz, dc = split_offset(slot)
    return STEPS.index((ZS - dz) % ZS) * (XS * CS) + ((XS - dx) % XS) * CS + dc


def hops(slot):
    dx, dz, dc = split_offset(slot)
    return min(dx, XS - dx) + min(dz, ZS - dz)


OTHERS = tuple(slot for slot in range(BLOCKS) if slot != OWN)
FARTHEST = tuple(sorted(OTHERS, key=hops, reverse=True))


def iota(shape, dim):
    return lax.broadcasted_iota(i32, shape, dim)


def dot(a, b, contract=((1,), (0,))):
    return lax.dot_general(a, b, (contract, ((), ())), preferred_element_type=f32)


def one_hot(mask):
    return jnp.where(mask, 1.0, 0.0).astype(bf16)


def narrow_hot(mask):
    return jnp.where(mask, jnp.ones((), bf16), jnp.zeros((), bf16))


def wait_for(buffer, sem):
    pltpu.make_async_copy(buffer, buffer, sem).wait()


def kernel(
    gal_far, nbt_far, q_far, lst_far,
    aug_ref, first_ref, final_ref,
    gal_ref, nbt_ref, q_ref, lst_ref, nbb, cums, counts, req_out, req_in, cols, sel, picked, arrived, pick, acc, augt, rows_t, lsb,
    lsq_out, lsq_in, ft_out, ft_in, rsq_out, rsq_in,
    part, part_in, half, half_in, piece, whole, esq_out, esq_in, fp_out, fp_in, esq_col,
    sem_in, send_req, recv_req, send_rep, recv_rep, send_y, recv_y, send_p, recv_p, send_e, recv_e,
):
    me = lax.axis_index("rows")
    my_y = lax.axis_index("rep")
    mx, mz, mc = me // (ZS * CS), (me // CS) % ZS, me % CS

    at_x = [((mx + dx) % XS) * (ZS * CS) for dx in range(XS)]
    at_z = [((mz + dz) % ZS) * CS for dz in range(ZS)]
    at_c = [(mc + dc) % CS for dc in range(CS)]

    def peer(slot):
        dx, dz, dc = split_offset(slot)
        return {"rows": at_x[dx] + at_z[dz] + at_c[dc]}

    def send(src, dst, s_sem, r_sem, target):
        pltpu.make_async_remote_copy(
            src_ref=src, dst_ref=dst, send_sem=s_sem, recv_sem=r_sem,
            device_id=target, device_id_type=MESH,
        ).start()

    pairs = ((nbt_far, nbt_ref), (gal_far, gal_ref), (q_far, q_ref), (lst_far, lst_ref))
    bring = [pltpu.make_async_copy(a, b, sem_in.at[i]) for i, (a, b) in enumerate(pairs)]
    for copy in bring:
        copy.start()
    barrier = pltpu.get_barrier_semaphore()

    for slot in FARTHEST:
        pl.semaphore_signal(barrier, inc=1, device_id=peer(slot), device_id_type=MESH)
    for e in range(1, YS):
        pl.semaphore_signal(
            barrier, inc=1, device_id={"rep": (my_y + e) % YS}, device_id_type=MESH
        )

    bring[0].wait()
    places = iota((256, ROWS), 0).astype(f32).astype(bf16)
    named = None
    for k in range(LINKS):
        row = nbt_ref[k : k + 1, :]
        low, high = [
            narrow_hot(places == part.astype(f32).astype(bf16)).astype(jnp.float8_e4m3fn)
            for part in (row & 255, row >> 8)
        ]
        found = dot(low, high, ((1,), (1,)))
        named = found if named is None else named + found

    def relative(high):
        block = high >> 2
        dx, dz, dc = ((block >> 4) - mx) & 3, ((block >> 1) - mz) & 7, (block - mc) & 1
        turn = sum(jnp.where(dz == step, at, 0) for at, step in enumerate(STEPS) if at)
        return (turn << 3) | (dx << 1) | dc

    high_row = iota((256, 256), 1)
    rel_row = relative(high_row)
    named = one_hot((named > 0.5) & (rel_row != OWN))
    up_to = one_hot(iota((256, 256), 1) <= iota((256, 256), 0))
    earlier = one_hot(
        ((iota((256, 256), 0) >> 2) == (iota((256, 256), 1) >> 2))
        & (iota((256, 256), 0) < iota((256, 256), 1))
    )
    before = dot(jnp.ones((256, 256), bf16), named).astype(bf16)
    cums[...] = dot(up_to, named) + dot(before, earlier)
    narrow = jnp.minimum(cums[...], 255.0).astype(bf16)
    for s in range(SLOTS):
        under = narrow_hot(narrow <= float(s))
        while under.shape[0] > 16:
            under = under[: under.shape[0] // 2] + under[under.shape[0] // 2 :]
        counts[pl.ds(s, 1), :] = jnp.sum(under.astype(f32), axis=0, keepdims=True)
    count = jnp.concatenate([counts[...].astype(bf16)] * 4, axis=0)
    to_row = one_hot(iota((BLOCKS, 256), 0) == relative(iota((BLOCKS, 256), 1)))
    asked = dot(to_row, count, ((1,), (1,)))
    for slot in OTHERS:
        req_out[slot] = asked[slot : slot + 1, :]

    pl.semaphore_wait(barrier, BLOCKS - 1 + YS - 1)

    for slot in FARTHEST:
        there = mirrored(slot)
        send(req_out.at[slot], req_in.at[there], send_req, recv_req.at[there // GROUP], peer(slot))

    wide = jnp.concatenate(
        [nbt_ref[...].astype(f32), jnp.zeros((128 - LINKS, ROWS), f32)], axis=0
    )
    for block in range(ROWS // 128):
        turned = jnp.transpose(wide[:, block * 128 : (block + 1) * 128]).astype(i32)
        for k in range(LINKS):
            nbb[k, block * 128 : (block + 1) * 128, :] = jnp.broadcast_to(
                turned[:, k : k + 1], (128, 128)
            )


    quarter_of = (relative(iota((128, 256), 1)) & 3) == (iota((128, 256), 0) >> 5)
    four = jnp.where(quarter_of, count.astype(f32), 0.0).astype(bf16)
    chunks = BLOCKS * SLOTS // 128
    to_chunk = one_hot(iota((chunks, 256), 0) == (relative(iota((chunks, 256), 1)) >> 2))
    offset = dot(to_chunk, four, ((1,), (1,))).astype(i32)
    slots = iota((chunks, 128), 0) * 4 + (iota((chunks, 128), 1) >> 5)
    dz = sum(jnp.where((slots >> 3) == at, step, 0) for at, step in enumerate(STEPS))
    owner = (
        ((((slots >> 1) & 3) + mx) & 3) * (ZS * CS) + ((dz + mz) & 7) * CS + ((slots + mc) & 1)
    )
    far_ids = jnp.where(offset < ROWS, owner * ROWS + offset, -1)
    near_ids = me * ROWS + iota((ROWS // 128, 128), 0) * 128 + iota((ROWS // 128, 128), 1)
    for c in range(ROWS // 128):
        cols[c] = jnp.broadcast_to(near_ids[c : c + 1, :], (8, 128))
    for c in range(chunks):
        cols[ROWS // 128 + c] = jnp.broadcast_to(far_ids[c : c + 1, :], (8, 128))
    arrived[OWN] = jnp.zeros((SLOTS, COLS), bf16)
    for copy in bring[1:]:
        copy.wait()

    for group in range(GROUPS):
        coming = GROUP - (OWN // GROUP == group)
        wait_for(req_in.at[pl.ds(group * GROUP, coming)], recv_req.at[group])
        wanted = [
            jnp.full((1, 128), float(ROWS), f32) if slot == OWN else req_in[slot]
            for slot in range(group * GROUP, (group + 1) * GROUP)
        ]
        wanted = jnp.transpose(jnp.concatenate(wanted, axis=0)).astype(i32)
        for j in range(GROUP):
            place = wanted[0:SLOTS, j : j + 1]
            pick[j * SLOTS : (j + 1) * SLOTS, :] = one_hot(iota((SLOTS, ROWS), 1) == place)
        taken = dot(pick[...], gal_ref[...]).astype(bf16)
        for j in range(GROUP):
            picked[group * GROUP + j] = taken[j * SLOTS : (j + 1) * SLOTS, :]
        for slot in range(group * GROUP, (group + 1) * GROUP):
            if slot != OWN:
                send(
                    picked.at[slot], arrived.at[mirrored(slot)], send_rep,
                    recv_rep.at[mirrored(slot) // GROUP], peer(slot),
                )

    def choose(block, carry):
        at = pl.multiple_of(block * 16, 16)
        ids = [nbb[k, pl.ds(at, 16), :] for k in range(LINKS)]
        for c in range(ROWS // 128 + chunks):
            column = cols[c]
            column = jnp.concatenate([column, column], axis=0)
            total = jnp.zeros((16, 128), f32)
            for k in range(LINKS):
                total = total + jnp.where(ids[k] == column, float(2 * LINKS - k), 0.0)
            sel[pl.ds(at, 16), c * 128 : (c + 1) * 128] = total.astype(bf16)
        return carry

    lax.fori_loop(0, ROWS // 16, choose, 0)
    acc[...] = float(2 * LINKS) * gal_ref[...].astype(f32)
    acc[...] += dot(sel[:, :ROWS], gal_ref[...])

    owned = lst_ref[...] >> 10
    inside = jnp.where(owned == me, lst_ref[...] & (ROWS - 1), -1)
    for k in range(LINKS):
        lsb[:, k * 128 : (k + 1) * 128] = one_hot(
            iota((ROWS, 128), 0) == inside[k : k + 1, :]
        )
    q_t = jnp.transpose(q_ref[...].astype(f32))
    query_sq = jnp.sum(q_t * q_t, axis=0, keepdims=True)

    for group in range(GROUPS):
        coming = GROUP - (OWN // GROUP == group)
        wait_for(arrived.at[pl.ds(group * GROUP, coming)], recv_rep.at[group])
        begin = ROWS + group * GROUP * SLOTS
        rows = arrived[group * GROUP : (group + 1) * GROUP].reshape(GROUP * SLOTS, COLS)
        acc[...] += dot(sel[:, begin : begin + GROUP * SLOTS], rows)

    augmented = (acc[...] * (1.0 / (2 * LINKS))).astype(bf16)
    aug_ref[...] = augmented
    aug_t = jnp.transpose(augmented.astype(f32))
    augt[...] = aug_t.astype(bf16)

    def y_peer(e):
        return {"rep": (my_y + e) % YS}

    lsq_out[...] = jnp.zeros_like(lsq_out)
    for k in range(0, LINKS, 2):
        pair = dot(augt[...], lsb[:, k * 128 : (k + 2) * 128])
        rows_t[:, k * 128 : (k + 2) * 128] = pair
        for j in range(2):
            rows = pair[:, j * 128 : (j + 1) * 128]
            lsq_out[k + j : k + j + 1, :] = jnp.sum(rows * q_t, axis=0, keepdims=True)
            lsq_out[LINKS + k + j : LINKS + k + j + 1, :] = jnp.sum(
                rows * rows, axis=0, keepdims=True
            )
    lsq_out[2 * LINKS : 2 * LINKS + 1, :] = query_sq
    for e in (2, 1, 3):
        send(lsq_out, lsq_in.at[YS - e], send_y.at[0], recv_y.at[0], y_peer(e))

    wait_for(lsq_in.at[pl.ds(1, YS - 1)], recv_y.at[0])
    sums = lsq_out[...] + lsq_in[1] + lsq_in[2] + lsq_in[3]
    q_scale = lax.rsqrt(sums[2 * LINKS : 2 * LINKS + 1, :] + epsilon)
    numer = jnp.zeros((COLS, QUERIES), f32)
    denom = jnp.zeros((1, QUERIES), f32)
    for k in range(LINKS):
        unit = lax.rsqrt(sums[LINKS + k : LINKS + k + 1, :] + epsilon)
        logit = logit_scale * sums[k : k + 1, :] * q_scale * unit
        weight = jnp.where(inside[k : k + 1, :] >= 0, jnp.exp(logit), 0.0)
        denom = denom + weight
        numer = numer + rows_t[:, k * 128 : (k + 1) * 128] * (weight * unit)

    def two_rows(total):
        high = total.astype(bf16).astype(f32)
        at = iota((TAIL, QUERIES), 0)
        return jnp.where(at == 0, high, jnp.where(at == 1, total - high, 0.0)).astype(bf16)

    slice_rows = COLS // (XS * CS)
    tail = two_rows(denom)
    for i in range(XS * CS):
        part[i, 0:slice_rows] = numer[i * slice_rows : (i + 1) * slice_rows, :].astype(bf16)
        part[i, slice_rows:] = tail
    mine = mx * CS + mc

    def near(e):
        ex, ec = e // CS, e % CS
        return (mx + ex) % XS, (mc + ec) % CS, ((XS - ex) % XS) * CS + ec

    order = (4, 5, 2, 3, 6, 7, 1)
    for e in order:
        px, pc, back = near(e)
        send(
            part.at[px * CS + pc], part_in.at[back], send_p.at[0], recv_p.at[0],
            {"rows": px * (ZS * CS) + mz * CS + pc},
        )
    wide_t = augt[...].astype(f32)
    rsq_out[...] = jnp.sum(wide_t * wide_t, axis=0, keepdims=True)
    first = dot(q_ref[...], augt[...])
    for y in range(YS):
        ft_out[y] = first[y * SHARE : (y + 1) * SHARE, :].astype(bf16)
    for e in (2, 1, 3):
        send(rsq_out, rsq_in.at[YS - e], send_y.at[1], recv_y.at[1], y_peer(e))
        send(ft_out.at[(my_y + e) % YS], ft_in.at[YS - e], send_y.at[2], recv_y.at[2], y_peer(e))

    wait_for(part_in.at[pl.ds(1, XS * CS - 1)], recv_p.at[0])
    so_far = part[mine].astype(f32)
    for e in range(1, XS * CS):
        so_far = so_far + part_in[e].astype(f32)
    half[0:slice_rows] = so_far[0:slice_rows].astype(bf16)
    half[slice_rows:] = two_rows(so_far[slice_rows : slice_rows + 1] + so_far[slice_rows + 1 : slice_rows + 2])
    for e in (4, 3, 5, 2, 6, 1, 7):
        send(
            half, half_in.at[ZS - e], send_p.at[1], recv_p.at[1],
            {"rows": mx * (ZS * CS) + ((mz + e) % ZS) * CS + mc},
        )

    wait_for(half_in.at[pl.ds(1, ZS - 1)], recv_p.at[1])
    so_far = half[...].astype(f32)
    for e in range(1, ZS):
        so_far = so_far + half_in[e].astype(f32)
    denom = so_far[slice_rows : slice_rows + 1] + so_far[slice_rows + 1 : slice_rows + 2]
    piece[...] = (so_far[0:slice_rows] / denom).astype(bf16)
    for e in order:
        px, pc, back = near(e)
        send(
            piece, whole.at[mine], send_p.at[2], recv_p.at[2],
            {"rows": px * (ZS * CS) + mz * CS + pc},
        )
    wait_for(rsq_in.at[pl.ds(1, YS - 1)], recv_y.at[1])
    wait_for(ft_in.at[pl.ds(1, YS - 1)], recv_y.at[2])
    row_scale = lax.rsqrt(rsq_out[...] + rsq_in[1] + rsq_in[2] + rsq_in[3] + epsilon)
    q_col = jnp.transpose(jnp.broadcast_to(q_scale * logit_scale, (QUERIES, QUERIES)))
    esq_col[...] = q_col
    mine_q = pl.ds(pl.multiple_of(my_y * SHARE, SHARE), SHARE)
    q_mine = esq_col[mine_q, 0:1]
    total = ft_out[my_y].astype(f32)
    for e in range(1, YS):
        total = total + ft_in[e].astype(f32)
    first_ref[...] = total * q_mine * row_scale

    wait_for(whole.at[pl.ds(1, XS * CS - 1)], recv_p.at[2])
    whole[mine] = piece[...]

    expanded_t = q_t * q_scale + whole[...].reshape(COLS, QUERIES).astype(f32)
    esq_out[...] = jnp.sum(expanded_t * expanded_t, axis=0, keepdims=True)
    expanded = jnp.transpose(expanded_t).astype(bf16)
    final = dot(expanded, augt[...])
    for y in range(YS):
        fp_out[y] = final[y * SHARE : (y + 1) * SHARE, :].astype(bf16)
    for e in (2, 1, 3):
        send(esq_out, esq_in.at[YS - e], send_e.at[0], recv_e.at[0], y_peer(e))
        send(fp_out.at[(my_y + e) % YS], fp_in.at[YS - e], send_e.at[1], recv_e.at[1], y_peer(e))
    wait_for(esq_in.at[pl.ds(1, YS - 1)], recv_e.at[0])
    e_scale = lax.rsqrt(esq_out[...] + esq_in[1] + esq_in[2] + esq_in[3] + epsilon)
    esq_col[...] = jnp.transpose(jnp.broadcast_to(e_scale * logit_scale, (QUERIES, QUERIES)))
    e_mine = esq_col[mine_q, 0:1]
    wait_for(fp_in.at[pl.ds(1, YS - 1)], recv_e.at[1])
    total = fp_out[my_y].astype(f32)
    for e in range(1, YS):
        total = total + fp_in[e].astype(f32)
    final_ref[...] = total * e_mine * row_scale

    wait_for(req_out.at[pl.ds(0, BLOCKS - 1)], send_req)
    wait_for(picked.at[pl.ds(0, BLOCKS - 1)], send_rep)
    wait_for(lsq_in.at[pl.ds(1, YS - 1)], send_y.at[0])
    wait_for(rsq_in.at[pl.ds(1, YS - 1)], send_y.at[1])
    wait_for(ft_in.at[pl.ds(1, YS - 1)], send_y.at[2])
    wait_for(part_in.at[pl.ds(1, XS * CS - 1)], send_p.at[0])
    wait_for(half_in.at[pl.ds(1, ZS - 1)], send_p.at[1])
    wait_for(whole.at[pl.ds(1, XS * CS - 1)], send_p.at[2])
    wait_for(esq_in.at[pl.ds(1, YS - 1)], send_e.at[0])
    wait_for(fp_in.at[pl.ds(1, YS - 1)], send_e.at[1])


def hand_over(aug_in, first_in, final_in, aug_out, first_out, final_out, sems):
    pairs = ((aug_in, aug_out), (first_in, first_out), (final_in, final_out))
    copies = [pltpu.make_async_copy(a, b, sems.at[i]) for i, (a, b) in enumerate(pairs)]
    for copy in copies:
        copy.start()
    for copy in copies:
        copy.wait()


def local(gallery, neighbours, queries, listed):
    vmem = pl.BlockSpec(memory_space=pltpu.VMEM)
    slice_rows = COLS // (XS * CS)
    columns = ROWS + BLOCKS * SLOTS
    dma = pltpu.SemaphoreType.DMA
    results = (
        jax.ShapeDtypeStruct((ROWS, COLS), bf16),
        jax.ShapeDtypeStruct((SHARE, ROWS), f32),
        jax.ShapeDtypeStruct((SHARE, ROWS), f32),
    )
    made = pl.pallas_call(
        kernel,
        out_shape=tuple(pltpu.VMEM(r.shape, r.dtype) for r in results),
        in_specs=[pl.BlockSpec(memory_space=pltpu.HBM)] * 4,
        out_specs=(vmem,) * 3,
        scratch_shapes=[
            pltpu.VMEM((ROWS, COLS), bf16),
            pltpu.VMEM((LINKS, ROWS), i32),
            pltpu.VMEM((QUERIES, COLS), bf16),
            pltpu.VMEM((LINKS, QUERIES), i32),
            pltpu.VMEM((LINKS, ROWS, 128), i32),
            pltpu.VMEM((256, 256), f32),
            pltpu.VMEM((SLOTS, 256), f32),
            pltpu.VMEM((BLOCKS, 1, 128), f32),
            pltpu.VMEM((BLOCKS, 1, 128), f32),
            pltpu.VMEM((columns // 128, 8, 128), i32),
            pltpu.VMEM((ROWS, columns), bf16),
            pltpu.VMEM((BLOCKS, SLOTS, COLS), bf16),
            pltpu.VMEM((BLOCKS, SLOTS, COLS), bf16),
            pltpu.VMEM((GROUP * SLOTS, ROWS), bf16),
            pltpu.VMEM((ROWS, COLS), f32),
            pltpu.VMEM((COLS, ROWS), bf16),
            pltpu.VMEM((COLS, LINKS * QUERIES), f32),
            pltpu.VMEM((ROWS, LINKS * QUERIES), bf16),
            pltpu.VMEM((24, QUERIES), f32),
            pltpu.VMEM((YS, 24, QUERIES), f32),
            pltpu.VMEM((YS, SHARE, ROWS), bf16),
            pltpu.VMEM((YS, SHARE, ROWS), bf16),
            pltpu.VMEM((1, ROWS), f32),
            pltpu.VMEM((YS, 1, ROWS), f32),
            pltpu.VMEM((XS * CS, slice_rows + TAIL, QUERIES), bf16),
            pltpu.VMEM((XS * CS, slice_rows + TAIL, QUERIES), bf16),
            pltpu.VMEM((slice_rows + TAIL, QUERIES), bf16),
            pltpu.VMEM((ZS, slice_rows + TAIL, QUERIES), bf16),
            pltpu.VMEM((slice_rows, QUERIES), bf16),
            pltpu.VMEM((XS * CS, slice_rows, QUERIES), bf16),
            pltpu.VMEM((1, QUERIES), f32),
            pltpu.VMEM((YS, 1, QUERIES), f32),
            pltpu.VMEM((YS, SHARE, ROWS), bf16),
            pltpu.VMEM((YS, SHARE, ROWS), bf16),
            pltpu.VMEM((QUERIES, QUERIES), f32),
            dma((4,)), dma, dma((GROUPS,)), dma, dma((GROUPS,)), dma((3,)), dma((3,)), dma((3,)), dma((3,)), dma((2,)), dma((2,)),
        ],
        compiler_params=pltpu.CompilerParams(
            collective_id=0, has_side_effects=True, vmem_limit_bytes=66100000
        ),
        name="expand",
    )(gallery, neighbours.T, queries, listed.T)
    return pl.pallas_call(
        hand_over,
        out_shape=results,
        in_specs=[vmem] * 3,
        out_specs=(pl.BlockSpec(memory_space=pl.ANY),) * 3,
        scratch_shapes=[dma((3,))],
        compiler_params=pltpu.CompilerParams(vmem_limit_bytes=4 * 1024 * 1024),
        name="hand_over",
    )(*made)


def solution(mesh):
    return jax.shard_map(
        local,
        mesh=mesh,
        in_specs=(P("rows", "rep"), P("rows", None), P(None, "rep"), P()),
        out_specs=(P("rows", "rep"), P("rep", "rows"), P("rep", "rows")),
        check_vma=False,
    )
```

```python
import jax
import jax.numpy as jnp
from jax import lax
from jax.experimental import pallas as pl
from jax.experimental.pallas import tpu as pltpu
from jax.sharding import PartitionSpec as P

epsilon = 1e-06
logit_scale = 32.0
MESH = pl.DeviceIdType.MESH
f32, bf16, i32 = jnp.float32, jnp.bfloat16, jnp.int32

ROWS = 1024
COLS = 256
LINKS = 10
SLOTS = 32
XS, ZS, CS, YS = 4, 8, 2, 4
BLOCKS = XS * ZS * CS
QUERIES = 128
SHARE = QUERIES // YS
GROUP = 8
GROUPS = BLOCKS // GROUP


STEPS = (1, 7, 4, 3, 5, 2, 6, 0)
OWN = (ZS - 1) * XS * CS


def split_offset(slot):
    return (slot // CS) % XS, STEPS[slot // (XS * CS)], slot % CS


def mirrored(slot):
    dx, dz, dc = split_offset(slot)
    return STEPS.index((ZS - dz) % ZS) * (XS * CS) + ((XS - dx) % XS) * CS + dc


def hops(slot):
    dx, dz, dc = split_offset(slot)
    return min(dx, XS - dx) + min(dz, ZS - dz)


OTHERS = tuple(slot for slot in range(BLOCKS) if slot != OWN)
FARTHEST = tuple(sorted(OTHERS, key=hops, reverse=True))


def iota(shape, dim):
    return lax.broadcasted_iota(i32, shape, dim)


def dot(a, b, contract=((1,), (0,))):
    return lax.dot_general(a, b, (contract, ((), ())), preferred_element_type=f32)


def one_hot(mask):
    return jnp.where(mask, 1.0, 0.0).astype(bf16)


def narrow_hot(mask):
    return jnp.where(mask, jnp.ones((), bf16), jnp.zeros((), bf16))


def wait_for(buffer, sem):
    pltpu.make_async_copy(buffer, buffer, sem).wait()


def kernel(
    gal_far, nbt_far, q_far, lst_far,
    aug_ref, first_ref, final_ref,
    gal_ref, nbt_ref, q_ref, lst_ref, nbb, cums, counts, req_out, req_in, cols, sel, picked, arrived, pick, acc, augt, rows_t, lsb,
    lsq_out, lsq_in, ft_out, ft_in, rsq_out, rsq_in,
    part, part_in, half, half_in, piece, whole, den_out, den_in, den_far, esq_out, esq_in, fp_out, fp_in, esq_col,
    sem_in, send_req, recv_req, send_rep, recv_rep, send_y, recv_y, send_p, recv_p, send_e, recv_e, send_d, recv_d,
):
    me = lax.axis_index("rows")
    my_y = lax.axis_index("rep")
    mx, mz, mc = me // (ZS * CS), (me // CS) % ZS, me % CS

    at_x = [((mx + dx) % XS) * (ZS * CS) for dx in range(XS)]
    at_z = [((mz + dz) % ZS) * CS for dz in range(ZS)]
    at_c = [(mc + dc) % CS for dc in range(CS)]

    def peer(slot):
        dx, dz, dc = split_offset(slot)
        return {"rows": at_x[dx] + at_z[dz] + at_c[dc]}

    def send(src, dst, s_sem, r_sem, target):
        pltpu.make_async_remote_copy(
            src_ref=src, dst_ref=dst, send_sem=s_sem, recv_sem=r_sem,
            device_id=target, device_id_type=MESH,
        ).start()

    pairs = ((nbt_far, nbt_ref), (gal_far, gal_ref), (q_far, q_ref), (lst_far, lst_ref))
    bring = [pltpu.make_async_copy(a, b, sem_in.at[i]) for i, (a, b) in enumerate(pairs)]
    for copy in bring:
        copy.start()
    barrier = pltpu.get_barrier_semaphore()

    for slot in FARTHEST:
        pl.semaphore_signal(barrier, inc=1, device_id=peer(slot), device_id_type=MESH)
    for e in range(1, YS):
        pl.semaphore_signal(
            barrier, inc=1, device_id={"rep": (my_y + e) % YS}, device_id_type=MESH
        )

    bring[0].wait()
    places = iota((256, ROWS), 0).astype(f32).astype(bf16)
    named = None
    for k in range(LINKS):
        row = nbt_ref[k : k + 1, :]
        low, high = [
            narrow_hot(places == part.astype(f32).astype(bf16)).astype(jnp.float8_e4m3fn)
            for part in (row & 255, row >> 8)
        ]
        found = dot(low, high, ((1,), (1,)))
        named = found if named is None else named + found

    def relative(high):
        block = high >> 2
        dx, dz, dc = ((block >> 4) - mx) & 3, ((block >> 1) - mz) & 7, (block - mc) & 1
        turn = sum(jnp.where(dz == step, at, 0) for at, step in enumerate(STEPS) if at)
        return (turn << 3) | (dx << 1) | dc

    high_row = iota((256, 256), 1)
    rel_row = relative(high_row)
    named = one_hot((named > 0.5) & (rel_row != OWN))
    up_to = one_hot(iota((256, 256), 1) <= iota((256, 256), 0))
    earlier = one_hot(
        ((iota((256, 256), 0) >> 2) == (iota((256, 256), 1) >> 2))
        & (iota((256, 256), 0) < iota((256, 256), 1))
    )
    before = dot(jnp.ones((256, 256), bf16), named).astype(bf16)
    cums[...] = dot(up_to, named) + dot(before, earlier)
    narrow = jnp.minimum(cums[...], 255.0).astype(bf16)
    for s in range(SLOTS):
        under = narrow_hot(narrow <= float(s))
        while under.shape[0] > 16:
            under = under[: under.shape[0] // 2] + under[under.shape[0] // 2 :]
        counts[pl.ds(s, 1), :] = jnp.sum(under.astype(f32), axis=0, keepdims=True)
    count = jnp.concatenate([counts[...].astype(bf16)] * 4, axis=0)
    to_row = one_hot(iota((BLOCKS, 256), 0) == relative(iota((BLOCKS, 256), 1)))
    asked = dot(to_row, count, ((1,), (1,)))
    for slot in OTHERS:
        req_out[slot] = asked[slot : slot + 1, :]

    pl.semaphore_wait(barrier, BLOCKS - 1 + YS - 1)

    for slot in FARTHEST:
        there = mirrored(slot)
        send(req_out.at[slot], req_in.at[there], send_req, recv_req.at[there // GROUP], peer(slot))

    wide = jnp.concatenate(
        [nbt_ref[...].astype(f32), jnp.zeros((128 - LINKS, ROWS), f32)], axis=0
    )
    for block in range(ROWS // 128):
        turned = jnp.transpose(wide[:, block * 128 : (block + 1) * 128]).astype(i32)
        for k in range(LINKS):
            nbb[k, block * 128 : (block + 1) * 128, :] = jnp.broadcast_to(
                turned[:, k : k + 1], (128, 128)
            )


    quarter_of = (relative(iota((128, 256), 1)) & 3) == (iota((128, 256), 0) >> 5)
    four = jnp.where(quarter_of, count.astype(f32), 0.0).astype(bf16)
    chunks = BLOCKS * SLOTS // 128
    to_chunk = one_hot(iota((chunks, 256), 0) == (relative(iota((chunks, 256), 1)) >> 2))
    offset = dot(to_chunk, four, ((1,), (1,))).astype(i32)
    slots = iota((chunks, 128), 0) * 4 + (iota((chunks, 128), 1) >> 5)
    dz = sum(jnp.where((slots >> 3) == at, step, 0) for at, step in enumerate(STEPS))
    owner = (
        ((((slots >> 1) & 3) + mx) & 3) * (ZS * CS) + ((dz + mz) & 7) * CS + ((slots + mc) & 1)
    )
    far_ids = jnp.where(offset < ROWS, owner * ROWS + offset, -1)
    near_ids = me * ROWS + iota((ROWS // 128, 128), 0) * 128 + iota((ROWS // 128, 128), 1)
    for c in range(ROWS // 128):
        cols[c] = jnp.broadcast_to(near_ids[c : c + 1, :], (8, 128))
    for c in range(chunks):
        cols[ROWS // 128 + c] = jnp.broadcast_to(far_ids[c : c + 1, :], (8, 128))
    arrived[OWN] = jnp.zeros((SLOTS, COLS), bf16)
    for copy in bring[1:]:
        copy.wait()

    for group in range(GROUPS):
        coming = GROUP - (OWN // GROUP == group)
        wait_for(req_in.at[pl.ds(group * GROUP, coming)], recv_req.at[group])
        wanted = [
            jnp.full((1, 128), float(ROWS), f32) if slot == OWN else req_in[slot]
            for slot in range(group * GROUP, (group + 1) * GROUP)
        ]
        wanted = jnp.transpose(jnp.concatenate(wanted, axis=0)).astype(i32)
        for j in range(GROUP):
            place = wanted[0:SLOTS, j : j + 1]
            pick[j * SLOTS : (j + 1) * SLOTS, :] = one_hot(iota((SLOTS, ROWS), 1) == place)
        taken = dot(pick[...], gal_ref[...]).astype(bf16)
        for j in range(GROUP):
            picked[group * GROUP + j] = taken[j * SLOTS : (j + 1) * SLOTS, :]
        for slot in range(group * GROUP, (group + 1) * GROUP):
            if slot != OWN:
                send(
                    picked.at[slot], arrived.at[mirrored(slot)], send_rep,
                    recv_rep.at[mirrored(slot) // GROUP], peer(slot),
                )

    def choose(block, carry):
        at = pl.multiple_of(block * 16, 16)
        ids = [nbb[k, pl.ds(at, 16), :] for k in range(LINKS)]
        for c in range(ROWS // 128 + chunks):
            column = cols[c]
            column = jnp.concatenate([column, column], axis=0)
            total = jnp.zeros((16, 128), f32)
            for k in range(LINKS):
                total = total + jnp.where(ids[k] == column, float(2 * LINKS - k), 0.0)
            sel[pl.ds(at, 16), c * 128 : (c + 1) * 128] = total.astype(bf16)
        return carry

    lax.fori_loop(0, ROWS // 16, choose, 0)
    gal_t = jnp.transpose(gal_ref[...].astype(f32))
    acc[...] = float(2 * LINKS) * gal_t
    acc[...] += dot(gal_t.astype(bf16), sel[:, :ROWS], ((1,), (1,)))

    owned = lst_ref[...] >> 10
    inside = jnp.where(owned == me, lst_ref[...] & (ROWS - 1), -1)
    for k in range(LINKS):
        lsb[:, k * 128 : (k + 1) * 128] = one_hot(
            iota((ROWS, 128), 0) == inside[k : k + 1, :]
        )
    q_t = jnp.transpose(q_ref[...].astype(f32))
    query_sq = jnp.sum(q_t * q_t, axis=0, keepdims=True)

    for group in range(GROUPS):
        coming = GROUP - (OWN // GROUP == group)
        wait_for(arrived.at[pl.ds(group * GROUP, coming)], recv_rep.at[group])
        begin = ROWS + group * GROUP * SLOTS
        rows = arrived[group * GROUP : (group + 1) * GROUP].reshape(GROUP * SLOTS, COLS)
        rows = jnp.transpose(rows.astype(f32)).astype(bf16)
        acc[...] += dot(rows, sel[:, begin : begin + GROUP * SLOTS], ((1,), (1,)))

    augt[...] = (acc[...] * (1.0 / (2 * LINKS))).astype(bf16)

    def y_peer(e):
        return {"rep": (my_y + e) % YS}

    lsq_out[...] = jnp.zeros_like(lsq_out)
    for k in range(0, LINKS, 2):
        pair = dot(augt[...], lsb[:, k * 128 : (k + 2) * 128])
        rows_t[:, k * 128 : (k + 2) * 128] = pair
        for j in range(2):
            rows = pair[:, j * 128 : (j + 1) * 128]
            lsq_out[k + j : k + j + 1, :] = jnp.sum(rows * q_t, axis=0, keepdims=True)
            lsq_out[LINKS + k + j : LINKS + k + j + 1, :] = jnp.sum(
                rows * rows, axis=0, keepdims=True
            )
    lsq_out[2 * LINKS : 2 * LINKS + 1, :] = query_sq
    for e in (2, 1, 3):
        send(lsq_out, lsq_in.at[YS - e], send_y.at[0], recv_y.at[0], y_peer(e))

    aug_ref[...] = jnp.transpose(augt[...].astype(f32)).astype(bf16)

    wait_for(lsq_in.at[pl.ds(1, YS - 1)], recv_y.at[0])
    sums = lsq_out[...] + lsq_in[1] + lsq_in[2] + lsq_in[3]
    q_scale = lax.rsqrt(sums[2 * LINKS : 2 * LINKS + 1, :] + epsilon)
    numer = jnp.zeros((COLS, QUERIES), f32)
    denom = jnp.zeros((1, QUERIES), f32)
    for k in range(LINKS):
        unit = lax.rsqrt(sums[LINKS + k : LINKS + k + 1, :] + epsilon)
        logit = logit_scale * sums[k : k + 1, :] * q_scale * unit
        weight = jnp.where(inside[k : k + 1, :] >= 0, jnp.exp(logit), 0.0)
        denom = denom + weight
        numer = numer + rows_t[:, k * 128 : (k + 1) * 128] * (weight * unit)

    slice_rows = COLS // (XS * CS)
    den_out[0] = denom
    for i in range(XS * CS):
        part[i] = numer[i * slice_rows : (i + 1) * slice_rows, :].astype(bf16)
    mine = mx * CS + mc

    def near(e):
        ex, ec = e // CS, e % CS
        return (mx + ex) % XS, (mc + ec) % CS, ((XS - ex) % XS) * CS + ec

    order = (4, 5, 2, 3, 6, 7, 1)
    for e in order:
        px, pc, back = near(e)
        send(
            den_out.at[0], den_in.at[back], send_d.at[0], recv_d.at[0],
            {"rows": px * (ZS * CS) + mz * CS + pc},
        )
        send(
            part.at[px * CS + pc], part_in.at[back], send_p.at[0], recv_p.at[0],
            {"rows": px * (ZS * CS) + mz * CS + pc},
        )
    wide_t = augt[...].astype(f32)
    rsq_out[...] = jnp.sum(wide_t * wide_t, axis=0, keepdims=True)
    first = dot(q_ref[...], augt[...])
    for y in range(YS):
        ft_out[y] = first[y * SHARE : (y + 1) * SHARE, :].astype(bf16)
    for e in (2, 1, 3):
        send(rsq_out, rsq_in.at[YS - e], send_y.at[1], recv_y.at[1], y_peer(e))
        send(ft_out.at[(my_y + e) % YS], ft_in.at[YS - e], send_y.at[2], recv_y.at[2], y_peer(e))

    wait_for(part_in.at[pl.ds(1, XS * CS - 1)], recv_p.at[0])
    so_far = part[mine].astype(f32)
    for e in range(1, XS * CS):
        so_far = so_far + part_in[e].astype(f32)
    half[...] = so_far.astype(bf16)
    wait_for(den_in.at[pl.ds(1, XS * CS - 1)], recv_d.at[0])
    den_out[1] = sum((den_in[e] for e in range(1, XS * CS)), den_out[0])
    for e in (4, 3, 5, 2, 6, 1, 7):
        send(
            den_out.at[1], den_far.at[ZS - e], send_d.at[1], recv_d.at[1],
            {"rows": mx * (ZS * CS) + ((mz + e) % ZS) * CS + mc},
        )
        send(
            half, half_in.at[ZS - e], send_p.at[1], recv_p.at[1],
            {"rows": mx * (ZS * CS) + ((mz + e) % ZS) * CS + mc},
        )

    wait_for(half_in.at[pl.ds(1, ZS - 1)], recv_p.at[1])
    so_far = half[...].astype(f32)
    for e in range(1, ZS):
        so_far = so_far + half_in[e].astype(f32)
    wait_for(den_far.at[pl.ds(1, ZS - 1)], recv_d.at[1])
    denom = sum((den_far[e] for e in range(1, ZS)), den_out[1])
    piece[...] = (so_far / denom).astype(bf16)
    for e in order:
        px, pc, back = near(e)
        send(
            piece, whole.at[mine], send_p.at[2], recv_p.at[2],
            {"rows": px * (ZS * CS) + mz * CS + pc},
        )
    wait_for(rsq_in.at[pl.ds(1, YS - 1)], recv_y.at[1])
    wait_for(ft_in.at[pl.ds(1, YS - 1)], recv_y.at[2])
    row_scale = lax.rsqrt(rsq_out[...] + rsq_in[1] + rsq_in[2] + rsq_in[3] + epsilon)
    q_col = jnp.transpose(jnp.broadcast_to(q_scale * logit_scale, (QUERIES, QUERIES)))
    esq_col[...] = q_col
    mine_q = pl.ds(pl.multiple_of(my_y * SHARE, SHARE), SHARE)
    q_mine = esq_col[mine_q, 0:1]
    total = ft_out[my_y].astype(f32)
    for e in range(1, YS):
        total = total + ft_in[e].astype(f32)
    first_ref[...] = total * q_mine * row_scale

    wait_for(whole.at[pl.ds(1, XS * CS - 1)], recv_p.at[2])
    whole[mine] = piece[...]

    expanded_t = q_t * q_scale + whole[...].reshape(COLS, QUERIES).astype(f32)
    esq_out[...] = jnp.sum(expanded_t * expanded_t, axis=0, keepdims=True)
    expanded = jnp.transpose(expanded_t).astype(bf16)
    final = dot(expanded, augt[...])
    for y in range(YS):
        fp_out[y] = final[y * SHARE : (y + 1) * SHARE, :].astype(bf16)
    for e in (2, 1, 3):
        send(esq_out, esq_in.at[YS - e], send_e.at[0], recv_e.at[0], y_peer(e))
        send(fp_out.at[(my_y + e) % YS], fp_in.at[YS - e], send_e.at[1], recv_e.at[1], y_peer(e))
    wait_for(esq_in.at[pl.ds(1, YS - 1)], recv_e.at[0])
    e_scale = lax.rsqrt(esq_out[...] + esq_in[1] + esq_in[2] + esq_in[3] + epsilon)
    esq_col[...] = jnp.transpose(jnp.broadcast_to(e_scale * logit_scale, (QUERIES, QUERIES)))
    e_mine = esq_col[mine_q, 0:1]
    wait_for(fp_in.at[pl.ds(1, YS - 1)], recv_e.at[1])
    total = fp_out[my_y].astype(f32)
    for e in range(1, YS):
        total = total + fp_in[e].astype(f32)
    final_ref[...] = total * e_mine * row_scale

    wait_for(req_out.at[pl.ds(0, BLOCKS - 1)], send_req)
    wait_for(picked.at[pl.ds(0, BLOCKS - 1)], send_rep)
    wait_for(lsq_in.at[pl.ds(1, YS - 1)], send_y.at[0])
    wait_for(rsq_in.at[pl.ds(1, YS - 1)], send_y.at[1])
    wait_for(ft_in.at[pl.ds(1, YS - 1)], send_y.at[2])
    wait_for(part_in.at[pl.ds(1, XS * CS - 1)], send_p.at[0])
    wait_for(half_in.at[pl.ds(1, ZS - 1)], send_p.at[1])
    wait_for(whole.at[pl.ds(1, XS * CS - 1)], send_p.at[2])
    wait_for(den_in.at[pl.ds(1, XS * CS - 1)], send_d.at[0])
    wait_for(den_far.at[pl.ds(1, ZS - 1)], send_d.at[1])
    wait_for(esq_in.at[pl.ds(1, YS - 1)], send_e.at[0])
    wait_for(fp_in.at[pl.ds(1, YS - 1)], send_e.at[1])


def hand_over(aug_in, first_in, final_in, aug_out, first_out, final_out, sems):
    pairs = ((aug_in, aug_out), (first_in, first_out), (final_in, final_out))
    copies = [pltpu.make_async_copy(a, b, sems.at[i]) for i, (a, b) in enumerate(pairs)]
    for copy in copies:
        copy.start()
    for copy in copies:
        copy.wait()


def local(gallery, neighbours, queries, listed):
    vmem = pl.BlockSpec(memory_space=pltpu.VMEM)
    slice_rows = COLS // (XS * CS)
    columns = ROWS + BLOCKS * SLOTS
    dma = pltpu.SemaphoreType.DMA
    results = (
        jax.ShapeDtypeStruct((ROWS, COLS), bf16),
        jax.ShapeDtypeStruct((SHARE, ROWS), f32),
        jax.ShapeDtypeStruct((SHARE, ROWS), f32),
    )
    made = pl.pallas_call(
        kernel,
        out_shape=tuple(pltpu.VMEM(r.shape, r.dtype) for r in results),
        in_specs=[pl.BlockSpec(memory_space=pltpu.HBM)] * 4,
        out_specs=(vmem,) * 3,
        scratch_shapes=[
            pltpu.VMEM((ROWS, COLS), bf16),
            pltpu.VMEM((LINKS, ROWS), i32),
            pltpu.VMEM((QUERIES, COLS), bf16),
            pltpu.VMEM((LINKS, QUERIES), i32),
            pltpu.VMEM((LINKS, ROWS, 128), i32),
            pltpu.VMEM((256, 256), f32),
            pltpu.VMEM((SLOTS, 256), f32),
            pltpu.VMEM((BLOCKS, 1, 128), f32),
            pltpu.VMEM((BLOCKS, 1, 128), f32),
            pltpu.VMEM((columns // 128, 8, 128), i32),
            pltpu.VMEM((ROWS, columns), bf16),
            pltpu.VMEM((BLOCKS, SLOTS, COLS), bf16),
            pltpu.VMEM((BLOCKS, SLOTS, COLS), bf16),
            pltpu.VMEM((GROUP * SLOTS, ROWS), bf16),
            pltpu.VMEM((COLS, ROWS), f32),
            pltpu.VMEM((COLS, ROWS), bf16),
            pltpu.VMEM((COLS, LINKS * QUERIES), f32),
            pltpu.VMEM((ROWS, LINKS * QUERIES), bf16),
            pltpu.VMEM((24, QUERIES), f32),
            pltpu.VMEM((YS, 24, QUERIES), f32),
            pltpu.VMEM((YS, SHARE, ROWS), bf16),
            pltpu.VMEM((YS, SHARE, ROWS), bf16),
            pltpu.VMEM((1, ROWS), f32),
            pltpu.VMEM((YS, 1, ROWS), f32),
            pltpu.VMEM((XS * CS, slice_rows, QUERIES), bf16),
            pltpu.VMEM((XS * CS, slice_rows, QUERIES), bf16),
            pltpu.VMEM((slice_rows, QUERIES), bf16),
            pltpu.VMEM((ZS, slice_rows, QUERIES), bf16),
            pltpu.VMEM((slice_rows, QUERIES), bf16),
            pltpu.VMEM((XS * CS, slice_rows, QUERIES), bf16),
            pltpu.VMEM((2, 1, QUERIES), f32),
            pltpu.VMEM((XS * CS, 1, QUERIES), f32),
            pltpu.VMEM((ZS, 1, QUERIES), f32),
            pltpu.VMEM((1, QUERIES), f32),
            pltpu.VMEM((YS, 1, QUERIES), f32),
            pltpu.VMEM((YS, SHARE, ROWS), bf16),
            pltpu.VMEM((YS, SHARE, ROWS), bf16),
            pltpu.VMEM((QUERIES, QUERIES), f32),
            dma((4,)), dma, dma((GROUPS,)), dma, dma((GROUPS,)), dma((3,)), dma((3,)), dma((3,)), dma((3,)), dma((2,)), dma((2,)), dma((2,)), dma((2,)),
        ],
        compiler_params=pltpu.CompilerParams(
            collective_id=0, has_side_effects=True, vmem_limit_bytes=66100000
        ),
        name="expand",
    )(gallery, neighbours.T, queries, listed.T)
    return pl.pallas_call(
        hand_over,
        out_shape=results,
        in_specs=[vmem] * 3,
        out_specs=(pl.BlockSpec(memory_space=pl.ANY),) * 3,
        scratch_shapes=[dma((3,))],
        compiler_params=pltpu.CompilerParams(vmem_limit_bytes=4 * 1024 * 1024),
        name="hand_over",
    )(*made)


def solution(mesh):
    return jax.shard_map(
        local,
        mesh=mesh,
        in_specs=(P("rows", "rep"), P("rows", None), P(None, "rep"), P()),
        out_specs=(P("rows", "rep"), P("rep", "rows"), P("rep", "rows")),
        check_vma=False,
    )
```

```python
import jax
import jax.numpy as jnp
from jax import lax
from jax.experimental import pallas as pl
from jax.experimental.pallas import tpu as pltpu
from jax.sharding import PartitionSpec as P

epsilon = 1e-06
logit_scale = 32.0
MESH = pl.DeviceIdType.MESH
f32, bf16, i32 = jnp.float32, jnp.bfloat16, jnp.int32

ROWS = 1024
COLS = 256
LINKS = 10
SLOTS = 32
XS, ZS, CS, YS = 4, 8, 2, 4
BLOCKS = XS * ZS * CS
QUERIES = 128
SHARE = QUERIES // YS
GROUP = 8
GROUPS = BLOCKS // GROUP


STEPS = (1, 7, 4, 3, 5, 2, 6, 0)
OWN = (ZS - 1) * XS * CS


def split_offset(slot):
    return (slot // CS) % XS, STEPS[slot // (XS * CS)], slot % CS


def mirrored(slot):
    dx, dz, dc = split_offset(slot)
    return STEPS.index((ZS - dz) % ZS) * (XS * CS) + ((XS - dx) % XS) * CS + dc


def hops(slot):
    dx, dz, dc = split_offset(slot)
    return min(dx, XS - dx) + min(dz, ZS - dz)


OTHERS = tuple(slot for slot in range(BLOCKS) if slot != OWN)
FARTHEST = tuple(sorted(OTHERS, key=hops, reverse=True))


def iota(shape, dim):
    return lax.broadcasted_iota(i32, shape, dim)


def dot(a, b, contract=((1,), (0,))):
    return lax.dot_general(a, b, (contract, ((), ())), preferred_element_type=f32)


def one_hot(mask):
    return jnp.where(mask, 1.0, 0.0).astype(bf16)


def narrow_hot(mask):
    return jnp.where(mask, jnp.ones((), bf16), jnp.zeros((), bf16))


def wait_for(buffer, sem):
    pltpu.make_async_copy(buffer, buffer, sem).wait()


def kernel(
    gal_far, nbt_far, q_far, lst_far,
    aug_ref, first_ref, final_ref,
    gal_ref, nbt_ref, q_ref, lst_ref, nbb, cums, counts, req_out, req_in, cols, sel, picked, arrived, pick, acc, augt, rows_t, lsb,
    lsq_out, lsq_in, ft_out, ft_in, rsq_out, rsq_in,
    part, part_in, half, half_in, piece, whole, den_out, den_in, den_far, esq_out, esq_in, fp_out, fp_in, esq_col,
    sem_in, send_req, recv_req, send_rep, recv_rep, send_y, recv_y, send_p, recv_p, send_e, recv_e, send_d, recv_d,
):
    me = lax.axis_index("rows")
    my_y = lax.axis_index("rep")
    mx, mz, mc = me // (ZS * CS), (me // CS) % ZS, me % CS

    at_x = [((mx + dx) % XS) * (ZS * CS) for dx in range(XS)]
    at_z = [((mz + dz) % ZS) * CS for dz in range(ZS)]
    at_c = [(mc + dc) % CS for dc in range(CS)]

    def peer(slot):
        dx, dz, dc = split_offset(slot)
        return {"rows": at_x[dx] + at_z[dz] + at_c[dc]}

    def send(src, dst, s_sem, r_sem, target):
        pltpu.make_async_remote_copy(
            src_ref=src, dst_ref=dst, send_sem=s_sem, recv_sem=r_sem,
            device_id=target, device_id_type=MESH,
        ).start()

    pairs = ((nbt_far, nbt_ref), (gal_far, gal_ref), (q_far, q_ref), (lst_far, lst_ref))
    bring = [pltpu.make_async_copy(a, b, sem_in.at[i]) for i, (a, b) in enumerate(pairs)]
    for copy in bring:
        copy.start()
    barrier = pltpu.get_barrier_semaphore()

    for slot in FARTHEST:
        pl.semaphore_signal(barrier, inc=1, device_id=peer(slot), device_id_type=MESH)
    for e in range(1, YS):
        pl.semaphore_signal(
            barrier, inc=1, device_id={"rep": (my_y + e) % YS}, device_id_type=MESH
        )

    bring[0].wait()
    places = iota((256, ROWS), 0).astype(f32).astype(bf16)
    named = None
    for k in range(LINKS):
        row = nbt_ref[k : k + 1, :]
        low, high = [
            narrow_hot(places == part.astype(f32).astype(bf16)).astype(jnp.float8_e4m3fn)
            for part in (row & 255, row >> 8)
        ]
        found = dot(low, high, ((1,), (1,)))
        named = found if named is None else named + found

    def relative(high):
        block = high >> 2
        dx, dz, dc = ((block >> 4) - mx) & 3, ((block >> 1) - mz) & 7, (block - mc) & 1
        turn = sum(jnp.where(dz == step, at, 0) for at, step in enumerate(STEPS) if at)
        return (turn << 3) | (dx << 1) | dc

    high_row = iota((256, 256), 1)
    rel_row = relative(high_row)
    named = one_hot((named > 0.5) & (rel_row != OWN))
    up_to = one_hot(iota((256, 256), 1) <= iota((256, 256), 0))
    earlier = one_hot(
        ((iota((256, 256), 0) >> 2) == (iota((256, 256), 1) >> 2))
        & (iota((256, 256), 0) < iota((256, 256), 1))
    )
    before = dot(jnp.ones((256, 256), bf16), named).astype(bf16)
    cums[...] = dot(up_to, named) + dot(before, earlier)
    narrow = jnp.minimum(cums[...], 255.0).astype(bf16)
    for s in range(SLOTS):
        under = narrow_hot(narrow <= float(s))
        while under.shape[0] > 16:
            under = under[: under.shape[0] // 2] + under[under.shape[0] // 2 :]
        counts[s * 16 : (s + 1) * 16, :] = under
    gather = narrow_hot(
        (iota((SLOTS, SLOTS * 16), 1) >> 4).astype(f32).astype(bf16)
        == iota((SLOTS, SLOTS * 16), 0).astype(f32).astype(bf16)
    )
    count = jnp.concatenate([dot(gather, counts[...]).astype(bf16)] * 4, axis=0)
    to_row = one_hot(iota((BLOCKS, 256), 0) == relative(iota((BLOCKS, 256), 1)))
    asked = dot(to_row, count, ((1,), (1,)))
    for slot in OTHERS:
        req_out[slot] = asked[slot : slot + 1, :]

    pl.semaphore_wait(barrier, BLOCKS - 1 + YS - 1)

    for slot in FARTHEST:
        there = mirrored(slot)
        send(req_out.at[slot], req_in.at[there], send_req, recv_req.at[there // GROUP], peer(slot))

    wide = jnp.concatenate(
        [nbt_ref[...].astype(f32), jnp.zeros((128 - LINKS, ROWS), f32)], axis=0
    )
    for block in range(ROWS // 128):
        turned = jnp.transpose(wide[:, block * 128 : (block + 1) * 128]).astype(i32)
        for k in range(LINKS):
            nbb[k, block * 128 : (block + 1) * 128, :] = jnp.broadcast_to(
                turned[:, k : k + 1], (128, 128)
            )


    quarter_of = (relative(iota((128, 256), 1)) & 3) == (iota((128, 256), 0) >> 5)
    four = jnp.where(quarter_of, count.astype(f32), 0.0).astype(bf16)
    chunks = BLOCKS * SLOTS // 128
    to_chunk = one_hot(iota((chunks, 256), 0) == (relative(iota((chunks, 256), 1)) >> 2))
    offset = dot(to_chunk, four, ((1,), (1,))).astype(i32)
    slots = iota((chunks, 128), 0) * 4 + (iota((chunks, 128), 1) >> 5)
    dz = sum(jnp.where((slots >> 3) == at, step, 0) for at, step in enumerate(STEPS))
    owner = (
        ((((slots >> 1) & 3) + mx) & 3) * (ZS * CS) + ((dz + mz) & 7) * CS + ((slots + mc) & 1)
    )
    far_ids = jnp.where(offset < ROWS, owner * ROWS + offset, -1)
    near_ids = me * ROWS + iota((ROWS // 128, 128), 0) * 128 + iota((ROWS // 128, 128), 1)
    for c in range(ROWS // 128):
        cols[c] = jnp.broadcast_to(near_ids[c : c + 1, :], (8, 128))
    for c in range(chunks):
        cols[ROWS // 128 + c] = jnp.broadcast_to(far_ids[c : c + 1, :], (8, 128))
    arrived[OWN] = jnp.zeros((SLOTS, COLS), bf16)
    for copy in bring[1:]:
        copy.wait()

    for group in range(GROUPS):
        coming = GROUP - (OWN // GROUP == group)
        wait_for(req_in.at[pl.ds(group * GROUP, coming)], recv_req.at[group])
        wanted = [
            jnp.full((1, 128), float(ROWS), f32) if slot == OWN else req_in[slot]
            for slot in range(group * GROUP, (group + 1) * GROUP)
        ]
        wanted = jnp.transpose(jnp.concatenate(wanted, axis=0)).astype(i32)
        for j in range(GROUP):
            place = wanted[0:SLOTS, j : j + 1]
            pick[j * SLOTS : (j + 1) * SLOTS, :] = one_hot(iota((SLOTS, ROWS), 1) == place)
        taken = dot(pick[...], gal_ref[...]).astype(bf16)
        for j in range(GROUP):
            picked[group * GROUP + j] = taken[j * SLOTS : (j + 1) * SLOTS, :]
        for slot in range(group * GROUP, (group + 1) * GROUP):
            if slot != OWN:
                send(
                    picked.at[slot], arrived.at[mirrored(slot)], send_rep,
                    recv_rep.at[mirrored(slot) // GROUP], peer(slot),
                )

    def choose(block, carry):
        at = pl.multiple_of(block * 16, 16)
        ids = [nbb[k, pl.ds(at, 16), :] for k in range(LINKS)]
        for c in range(ROWS // 128 + chunks):
            column = cols[c]
            column = jnp.concatenate([column, column], axis=0)
            total = jnp.zeros((16, 128), f32)
            for k in range(LINKS):
                total = total + jnp.where(ids[k] == column, float(2 * LINKS - k), 0.0)
            sel[pl.ds(at, 16), c * 128 : (c + 1) * 128] = total.astype(bf16)
        return carry

    lax.fori_loop(0, ROWS // 16, choose, 0)
    gal_t = jnp.transpose(gal_ref[...].astype(f32))
    acc[...] = float(2 * LINKS) * gal_t
    acc[...] += dot(gal_t.astype(bf16), sel[:, :ROWS], ((1,), (1,)))

    owned = lst_ref[...] >> 10
    inside = jnp.where(owned == me, lst_ref[...] & (ROWS - 1), -1)
    for k in range(LINKS):
        lsb[:, k * 128 : (k + 1) * 128] = one_hot(
            iota((ROWS, 128), 0) == inside[k : k + 1, :]
        )
    q_t = jnp.transpose(q_ref[...].astype(f32))
    query_sq = jnp.sum(q_t * q_t, axis=0, keepdims=True)

    for group in range(GROUPS):
        coming = GROUP - (OWN // GROUP == group)
        wait_for(arrived.at[pl.ds(group * GROUP, coming)], recv_rep.at[group])
        begin = ROWS + group * GROUP * SLOTS
        rows = arrived[group * GROUP : (group + 1) * GROUP].reshape(GROUP * SLOTS, COLS)
        rows = jnp.transpose(rows.astype(f32)).astype(bf16)
        acc[...] += dot(rows, sel[:, begin : begin + GROUP * SLOTS], ((1,), (1,)))

    augt[...] = (acc[...] * (1.0 / (2 * LINKS))).astype(bf16)

    def y_peer(e):
        return {"rep": (my_y + e) % YS}

    lsq_out[...] = jnp.zeros_like(lsq_out)
    for k in range(0, LINKS, 2):
        pair = dot(augt[...], lsb[:, k * 128 : (k + 2) * 128])
        rows_t[:, k * 128 : (k + 2) * 128] = pair
        for j in range(2):
            rows = pair[:, j * 128 : (j + 1) * 128]
            lsq_out[k + j : k + j + 1, :] = jnp.sum(rows * q_t, axis=0, keepdims=True)
            lsq_out[LINKS + k + j : LINKS + k + j + 1, :] = jnp.sum(
                rows * rows, axis=0, keepdims=True
            )
    lsq_out[2 * LINKS : 2 * LINKS + 1, :] = query_sq
    for e in (2, 1, 3):
        send(lsq_out, lsq_in.at[YS - e], send_y.at[0], recv_y.at[0], y_peer(e))

    aug_ref[...] = jnp.transpose(augt[...].astype(f32)).astype(bf16)

    wait_for(lsq_in.at[pl.ds(1, YS - 1)], recv_y.at[0])
    sums = lsq_out[...] + lsq_in[1] + lsq_in[2] + lsq_in[3]
    q_scale = lax.rsqrt(sums[2 * LINKS : 2 * LINKS + 1, :] + epsilon)
    numer = jnp.zeros((COLS, QUERIES), f32)
    denom = jnp.zeros((1, QUERIES), f32)
    for k in range(LINKS):
        unit = lax.rsqrt(sums[LINKS + k : LINKS + k + 1, :] + epsilon)
        logit = logit_scale * sums[k : k + 1, :] * q_scale * unit
        weight = jnp.where(inside[k : k + 1, :] >= 0, jnp.exp(logit), 0.0)
        denom = denom + weight
        numer = numer + rows_t[:, k * 128 : (k + 1) * 128] * (weight * unit)

    slice_rows = COLS // (XS * CS)
    den_out[0] = denom
    for i in range(XS * CS):
        part[i] = numer[i * slice_rows : (i + 1) * slice_rows, :].astype(bf16)
    mine = mx * CS + mc

    def near(e):
        ex, ec = e // CS, e % CS
        return (mx + ex) % XS, (mc + ec) % CS, ((XS - ex) % XS) * CS + ec

    order = (4, 5, 2, 3, 6, 7, 1)
    for e in order:
        px, pc, back = near(e)
        send(
            den_out.at[0], den_in.at[back], send_d.at[0], recv_d.at[0],
            {"rows": px * (ZS * CS) + mz * CS + pc},
        )
        send(
            part.at[px * CS + pc], part_in.at[back], send_p.at[0], recv_p.at[0],
            {"rows": px * (ZS * CS) + mz * CS + pc},
        )
    wide_t = augt[...].astype(f32)
    rsq_out[...] = jnp.sum(wide_t * wide_t, axis=0, keepdims=True)
    first = dot(q_ref[...], augt[...])
    for y in range(YS):
        ft_out[y] = first[y * SHARE : (y + 1) * SHARE, :].astype(bf16)
    for e in (2, 1, 3):
        send(rsq_out, rsq_in.at[YS - e], send_y.at[1], recv_y.at[1], y_peer(e))
        send(ft_out.at[(my_y + e) % YS], ft_in.at[YS - e], send_y.at[2], recv_y.at[2], y_peer(e))

    wait_for(part_in.at[pl.ds(1, XS * CS - 1)], recv_p.at[0])
    so_far = part[mine].astype(f32)
    for e in range(1, XS * CS):
        so_far = so_far + part_in[e].astype(f32)
    half[...] = so_far.astype(bf16)
    wait_for(den_in.at[pl.ds(1, XS * CS - 1)], recv_d.at[0])
    den_out[1] = sum((den_in[e] for e in range(1, XS * CS)), den_out[0])
    for e in (4, 3, 5, 2, 6, 1, 7):
        send(
            den_out.at[1], den_far.at[ZS - e], send_d.at[1], recv_d.at[1],
            {"rows": mx * (ZS * CS) + ((mz + e) % ZS) * CS + mc},
        )
        send(
            half, half_in.at[ZS - e], send_p.at[1], recv_p.at[1],
            {"rows": mx * (ZS * CS) + ((mz + e) % ZS) * CS + mc},
        )

    wait_for(half_in.at[pl.ds(1, ZS - 1)], recv_p.at[1])
    so_far = half[...].astype(f32)
    for e in range(1, ZS):
        so_far = so_far + half_in[e].astype(f32)
    wait_for(den_far.at[pl.ds(1, ZS - 1)], recv_d.at[1])
    denom = sum((den_far[e] for e in range(1, ZS)), den_out[1])
    piece[...] = (so_far / denom).astype(bf16)
    for e in order:
        px, pc, back = near(e)
        send(
            piece, whole.at[mine], send_p.at[2], recv_p.at[2],
            {"rows": px * (ZS * CS) + mz * CS + pc},
        )
    wait_for(rsq_in.at[pl.ds(1, YS - 1)], recv_y.at[1])
    wait_for(ft_in.at[pl.ds(1, YS - 1)], recv_y.at[2])
    row_scale = lax.rsqrt(rsq_out[...] + rsq_in[1] + rsq_in[2] + rsq_in[3] + epsilon)
    q_col = jnp.transpose(jnp.broadcast_to(q_scale * logit_scale, (QUERIES, QUERIES)))
    esq_col[...] = q_col
    mine_q = pl.ds(pl.multiple_of(my_y * SHARE, SHARE), SHARE)
    q_mine = esq_col[mine_q, 0:1]
    total = ft_out[my_y].astype(f32)
    for e in range(1, YS):
        total = total + ft_in[e].astype(f32)
    first_ref[...] = total * q_mine * row_scale

    wait_for(whole.at[pl.ds(1, XS * CS - 1)], recv_p.at[2])
    whole[mine] = piece[...]

    expanded_t = q_t * q_scale + whole[...].reshape(COLS, QUERIES).astype(f32)
    esq_out[...] = jnp.sum(expanded_t * expanded_t, axis=0, keepdims=True)
    expanded = jnp.transpose(expanded_t).astype(bf16)
    final = dot(expanded, augt[...])
    for y in range(YS):
        fp_out[y] = final[y * SHARE : (y + 1) * SHARE, :].astype(bf16)
    for e in (2, 1, 3):
        send(esq_out, esq_in.at[YS - e], send_e.at[0], recv_e.at[0], y_peer(e))
        send(fp_out.at[(my_y + e) % YS], fp_in.at[YS - e], send_e.at[1], recv_e.at[1], y_peer(e))
    wait_for(esq_in.at[pl.ds(1, YS - 1)], recv_e.at[0])
    e_scale = lax.rsqrt(esq_out[...] + esq_in[1] + esq_in[2] + esq_in[3] + epsilon)
    esq_col[...] = jnp.transpose(jnp.broadcast_to(e_scale * logit_scale, (QUERIES, QUERIES)))
    e_mine = esq_col[mine_q, 0:1]
    wait_for(fp_in.at[pl.ds(1, YS - 1)], recv_e.at[1])
    total = fp_out[my_y].astype(f32)
    for e in range(1, YS):
        total = total + fp_in[e].astype(f32)
    final_ref[...] = total * e_mine * row_scale

    wait_for(req_out.at[pl.ds(0, BLOCKS - 1)], send_req)
    wait_for(picked.at[pl.ds(0, BLOCKS - 1)], send_rep)
    wait_for(lsq_in.at[pl.ds(1, YS - 1)], send_y.at[0])
    wait_for(rsq_in.at[pl.ds(1, YS - 1)], send_y.at[1])
    wait_for(ft_in.at[pl.ds(1, YS - 1)], send_y.at[2])
    wait_for(part_in.at[pl.ds(1, XS * CS - 1)], send_p.at[0])
    wait_for(half_in.at[pl.ds(1, ZS - 1)], send_p.at[1])
    wait_for(whole.at[pl.ds(1, XS * CS - 1)], send_p.at[2])
    wait_for(den_in.at[pl.ds(1, XS * CS - 1)], send_d.at[0])
    wait_for(den_far.at[pl.ds(1, ZS - 1)], send_d.at[1])
    wait_for(esq_in.at[pl.ds(1, YS - 1)], send_e.at[0])
    wait_for(fp_in.at[pl.ds(1, YS - 1)], send_e.at[1])


def hand_over(aug_in, first_in, final_in, aug_out, first_out, final_out, sems):
    pairs = ((aug_in, aug_out), (first_in, first_out), (final_in, final_out))
    copies = [pltpu.make_async_copy(a, b, sems.at[i]) for i, (a, b) in enumerate(pairs)]
    for copy in copies:
        copy.start()
    for copy in copies:
        copy.wait()


def local(gallery, neighbours, queries, listed):
    vmem = pl.BlockSpec(memory_space=pltpu.VMEM)
    slice_rows = COLS // (XS * CS)
    columns = ROWS + BLOCKS * SLOTS
    dma = pltpu.SemaphoreType.DMA
    results = (
        jax.ShapeDtypeStruct((ROWS, COLS), bf16),
        jax.ShapeDtypeStruct((SHARE, ROWS), f32),
        jax.ShapeDtypeStruct((SHARE, ROWS), f32),
    )
    made = pl.pallas_call(
        kernel,
        out_shape=tuple(pltpu.VMEM(r.shape, r.dtype) for r in results),
        in_specs=[pl.BlockSpec(memory_space=pltpu.HBM)] * 4,
        out_specs=(vmem,) * 3,
        scratch_shapes=[
            pltpu.VMEM((ROWS, COLS), bf16),
            pltpu.VMEM((LINKS, ROWS), i32),
            pltpu.VMEM((QUERIES, COLS), bf16),
            pltpu.VMEM((LINKS, QUERIES), i32),
            pltpu.VMEM((LINKS, ROWS, 128), i32),
            pltpu.VMEM((256, 256), f32),
            pltpu.VMEM((SLOTS * 16, 256), bf16),
            pltpu.VMEM((BLOCKS, 1, 128), f32),
            pltpu.VMEM((BLOCKS, 1, 128), f32),
            pltpu.VMEM((columns // 128, 8, 128), i32),
            pltpu.VMEM((ROWS, columns), bf16),
            pltpu.VMEM((BLOCKS, SLOTS, COLS), bf16),
            pltpu.VMEM((BLOCKS, SLOTS, COLS), bf16),
            pltpu.VMEM((GROUP * SLOTS, ROWS), bf16),
            pltpu.VMEM((COLS, ROWS), f32),
            pltpu.VMEM((COLS, ROWS), bf16),
            pltpu.VMEM((COLS, LINKS * QUERIES), f32),
            pltpu.VMEM((ROWS, LINKS * QUERIES), bf16),
            pltpu.VMEM((24, QUERIES), f32),
            pltpu.VMEM((YS, 24, QUERIES), f32),
            pltpu.VMEM((YS, SHARE, ROWS), bf16),
            pltpu.VMEM((YS, SHARE, ROWS), bf16),
            pltpu.VMEM((1, ROWS), f32),
            pltpu.VMEM((YS, 1, ROWS), f32),
            pltpu.VMEM((XS * CS, slice_rows, QUERIES), bf16),
            pltpu.VMEM((XS * CS, slice_rows, QUERIES), bf16),
            pltpu.VMEM((slice_rows, QUERIES), bf16),
            pltpu.VMEM((ZS, slice_rows, QUERIES), bf16),
            pltpu.VMEM((slice_rows, QUERIES), bf16),
            pltpu.VMEM((XS * CS, slice_rows, QUERIES), bf16),
            pltpu.VMEM((2, 1, QUERIES), f32),
            pltpu.VMEM((XS * CS, 1, QUERIES), f32),
            pltpu.VMEM((ZS, 1, QUERIES), f32),
            pltpu.VMEM((1, QUERIES), f32),
            pltpu.VMEM((YS, 1, QUERIES), f32),
            pltpu.VMEM((YS, SHARE, ROWS), bf16),
            pltpu.VMEM((YS, SHARE, ROWS), bf16),
            pltpu.VMEM((QUERIES, QUERIES), f32),
            dma((4,)), dma, dma((GROUPS,)), dma, dma((GROUPS,)), dma((3,)), dma((3,)), dma((3,)), dma((3,)), dma((2,)), dma((2,)), dma((2,)), dma((2,)),
        ],
        compiler_params=pltpu.CompilerParams(
            collective_id=0, has_side_effects=True, vmem_limit_bytes=66100000
        ),
        name="expand",
    )(gallery, neighbours.T, queries, listed.T)
    return pl.pallas_call(
        hand_over,
        out_shape=results,
        in_specs=[vmem] * 3,
        out_specs=(pl.BlockSpec(memory_space=pl.ANY),) * 3,
        scratch_shapes=[dma((3,))],
        compiler_params=pltpu.CompilerParams(vmem_limit_bytes=4 * 1024 * 1024),
        name="hand_over",
    )(*made)


def solution(mesh):
    return jax.shard_map(
        local,
        mesh=mesh,
        in_specs=(P("rows", "rep"), P("rows", None), P(None, "rep"), P()),
        out_specs=(P("rows", "rep"), P("rep", "rows"), P("rep", "rows")),
        check_vma=False,
    )
```
